32 devices in a mesh: ctx: 8 (over z, x), heads: 4 (over y, core).
Axes of the slice: x: 2, y: 2, z: 4, core: 2. Of those that a mesh axis runs over, the one named last changes fastest.
Arguments:
- activations: bfloat16 [2048, 8192], P('ctx', 'heads'), may hold values from -20 to 20
- w_query: bfloat16 [8192, 4096], P(None, 'heads'), may hold values from -0.0625 to 0.0625
- w_key: bfloat16 [8192, 1024], P(None, 'heads'), may hold values from -0.0625 to 0.0625
- w_value: bfloat16 [8192, 1024], P(None, 'heads'), may hold values from -0.0625 to 0.0625
- doc_lengths: int32 [8], replicated, may hold values from 1 to 1024, 2048 in all
- block_dest: int32 [32], replicated, may hold values from 0 to 7, as said below
- out_grad: bfloat16 [2048, 4096], P('ctx', 'heads'), may hold values from -6 to 6
Outputs:
- attention: bfloat16 [2048, 4096], P('ctx', 'heads')
- input_grad: bfloat16 [2048, 8192], P('ctx', 'heads')
The draws below stay inside these ranges and needn't reach their ends.
Inputs may be any that keep to these rules, and one draw needn't show every extreme that they name: `block_dest`: loader block b lies on loader shard b // 4. Each loader shard sends its blocks to different context shards, and each context shard receives exactly 4 blocks, from different loader shards.
All inputs are finite; a program needn't handle non-finite values.
Results may differ from the reference program's by a relative error of at most 0.025.
The reference program's roundings to bfloat16 on the way count: a program that leaves them out, or rounds other values in their place, can miss the bound.
Values may be sent and summed in bfloat16 or wider, within the bound.
A program may use at most 128 MiB of HBM per device.

```python
import math
import jax
import jax.numpy as jnp
import numpy as np
from jax import lax

D = 8192
KVH = 8
HD = 128
QPK = 4
NDOC = 8
TOK_DEV = 256
BLK = 64
TOKENS = 2048
QH = 32


def draw_activations(key, part):
    entries = jnp.clip(jax.random.normal(key, (TOKENS, D), jnp.float32), -6.0, 6.0)
    return entries.astype(jnp.bfloat16)


def draw_block_dest(key, part):
    shards = TOKENS // TOK_DEV
    blocks_each = TOK_DEV // BLK
    first, second, third = jax.random.split(jax.random.fold_in(key, 17), 3)
    perm_rows = jax.random.permutation(first, shards).astype(jnp.int32)
    perm_cols = jax.random.permutation(second, shards).astype(jnp.int32)
    offsets = jax.random.permutation(third, shards).astype(jnp.int32)[:blocks_each]
    cells = jnp.mod(perm_rows[:, None] + offsets[None, :], shards)
    return perm_cols[cells].reshape(-1).astype(jnp.int32)


def shard_levels(key, extent, pieces, low, high):
    level = 1.0
    for dim, blocks in pieces:
        steps = jax.random.uniform(jax.random.fold_in(jax.random.fold_in(key, 6), dim), (blocks,), jnp.float32, low / len(pieces), high / len(pieces))
        level = level * jnp.repeat(jnp.exp(steps), extent[dim] // blocks).reshape((-1,) + (1,) * (len(extent) - 1 - dim))
    return level


def length_profile(count, total, reach, skew):
    loads = [(1 << 20) // math.isqrt(standing ** skew) + 1 for standing in range(2, count + 1)]
    spare, holding = total - reach - (count - 1), [1] * (count - 1)
    while spare > 0:
        free = [i for i in range(count - 1) if holding[i] < reach]
        whole, budget = sum([loads[i] for i in free]), spare
        for i in free:
            extra = min(reach - holding[i], max(1, budget * loads[i] // whole), spare)
            holding[i] = holding[i] + extra
            spare = spare - extra
    return np.array([reach] + holding)


def ragged(own_key, number_of, total, limit, lean):
    if number_of == 2:
        one = jax.random.randint(own_key, (), max(1, total - limit), min(limit, total - 1) + 1)
        return jnp.stack([one, total - one])
    sizes = jnp.asarray(length_profile(number_of, total, limit, lean), jnp.int32)
    twos = (number_of - 1) // 2
    giver, taker = sizes[1:1 + 2 * twos:2], sizes[2:2 + 2 * twos:2]
    slack = jnp.minimum(giver - 1, limit - taker)
    moved = jax.random.randint(jax.random.fold_in(own_key, 1), (twos,), 0, 1 << 20) % (slack + 1)
    sizes = sizes.at[1:1 + 2 * twos:2].set(giver - moved).at[2:2 + 2 * twos:2].set(taker + moved)
    return sizes[jax.random.permutation(jax.random.fold_in(own_key, 2), number_of)]


def centred(stream_key, extent, width, limit, pieces=(), kind=jnp.bfloat16):
    drawn = width * jax.random.normal(stream_key, extent, jnp.float32)
    if pieces:
        drawn = drawn * shard_levels(stream_key, extent, pieces, -0.22, 0.18)
    return jnp.clip(drawn, -limit, limit).astype(kind)


def setup_inputs(seed: int = 0) -> dict:
    key_list = jax.random.split(jax.random.key(seed), 8)
    return {
        "activations": draw_activations(jax.random.fold_in(key_list[7], 71), 0),
        "w_query": centred(key_list[1], (D, QH * HD), D ** -0.5, 0.0625, ((1, 4),)),
        "w_key": centred(key_list[2], (D, KVH * HD), D ** -0.5, 0.0625, ((1, 4),)),
        "w_value": centred(key_list[3], (D, KVH * HD), D ** -0.5, 0.0625, ((1, 4),)),
        "doc_lengths": ragged(key_list[4], NDOC, TOKENS, TOKENS // 2, 2).astype(jnp.int32),
        "block_dest": draw_block_dest(jax.random.fold_in(key_list[7], 71), 0),
        "out_grad": centred(key_list[6], (TOKENS, QH * HD), 1.0, 6.0, ((0, 8), (1, 4))),
    }


NEG = -1e+30

def layout(block_dest):
    nblk = block_dest.shape[0]
    index = jnp.arange(nblk, dtype=jnp.int32)
    order_key = block_dest.astype(jnp.int32) * nblk + index
    ranks = lax.optimization_barrier(jnp.sum((order_key[None, :] < order_key[:, None]).astype(jnp.int32), axis=1))
    ctx_blocks = lax.optimization_barrier(jnp.sum(jnp.where(ranks[None, :] == index[:, None], index[None, :], 0), axis=1)).astype(jnp.int32)
    ctx_pos = (ctx_blocks[:, None] * BLK + jnp.arange(BLK, dtype=jnp.int32)[None, :]).reshape(-1)
    return (ctx_blocks, ctx_pos)

def doc_ids(positions, doc_lengths):
    ends = jnp.cumsum(doc_lengths.astype(jnp.int32)).astype(jnp.int32)
    return lax.optimization_barrier(jnp.sum((ends[None, :] <= positions[:, None]).astype(jnp.int32), axis=1)).astype(jnp.int32)

def reference(activations, w_query, w_key, w_value, doc_lengths, block_dest, out_grad):
    scale = 1.0 / math.sqrt(HD)
    queries = jnp.dot(activations, w_query, preferred_element_type=jnp.float32).astype(jnp.bfloat16)
    keys = jnp.dot(activations, w_key, preferred_element_type=jnp.float32).astype(jnp.bfloat16)
    values = jnp.dot(activations, w_value, preferred_element_type=jnp.float32).astype(jnp.bfloat16)
    ctx_blocks, ctx_pos = layout(block_dest)
    loader_pos = jnp.arange(TOKENS, dtype=jnp.int32)
    docs = doc_ids(loader_pos, doc_lengths)
    visible = (docs[None, :] == docs[:, None]) & (loader_pos[None, :] <= loader_pos[:, None])
    grad_loader = jnp.zeros_like(out_grad).at[ctx_pos].set(out_grad)
    query_g = queries.reshape(TOKENS, KVH, QPK, HD).transpose(1, 0, 2, 3)
    key_g = keys.reshape(TOKENS, KVH, HD).transpose(1, 0, 2)
    value_g = values.reshape(TOKENS, KVH, HD).transpose(1, 0, 2)
    grad_g = grad_loader.reshape(TOKENS, KVH, QPK, HD).transpose(1, 0, 2, 3)

    def one_group(operands):
        query_h, key_h, value_h, grad_h = operands
        query_f = query_h.astype(jnp.float32)
        key_f = key_h.astype(jnp.float32)
        value_f = value_h.astype(jnp.float32)
        grad_f = grad_h.astype(jnp.float32)
        scores = jnp.einsum('tqe,se->qts', query_f, key_f) * scale
        masked = jnp.where(visible[None], scores, NEG)
        top = lax.optimization_barrier(jnp.max(masked, axis=-1, keepdims=True))
        total = lax.optimization_barrier(jnp.sum(jnp.where(visible[None], jnp.exp(masked - top), 0.0), axis=-1, keepdims=True))
        lse = top + jnp.log(total)
        weights = jnp.where(visible[None], jnp.exp(scores - lse), 0.0)
        weights_b = lax.optimization_barrier(weights.astype(jnp.bfloat16)).astype(jnp.float32)
        attn = jnp.einsum('qts,se->tqe', weights, value_f, precision=lax.Precision.HIGHEST).astype(jnp.bfloat16)
        delta = lax.optimization_barrier(jnp.sum(grad_f * attn.astype(jnp.float32), axis=-1))
        dvalue = jnp.einsum('qts,tqe->se', weights_b, grad_f)
        dprob = jnp.einsum('tqe,se->qts', grad_f, value_f)
        dscore = (weights * (dprob - delta.T[:, :, None]) * scale).astype(jnp.bfloat16)
        dscore_f = lax.optimization_barrier(dscore).astype(jnp.float32)
        dquery = jnp.einsum('qts,se->tqe', dscore_f, key_f)
        dkey = jnp.einsum('qts,tqe->se', dscore_f, query_f)
        return (attn, dquery.astype(jnp.bfloat16), dkey.astype(jnp.bfloat16), dvalue.astype(jnp.bfloat16))
    attn_g, dquery_g, dkey_g, dvalue_g = lax.map(one_group, (query_g, key_g, value_g, grad_g))
    attn_loader = attn_g.transpose(1, 0, 2, 3).reshape(TOKENS, QH * HD)
    attention = attn_loader[ctx_pos]
    dquery = dquery_g.transpose(1, 0, 2, 3).reshape(TOKENS, QH * HD)
    dkey = dkey_g.transpose(1, 0, 2).reshape(TOKENS, KVH * HD)
    dvalue = dvalue_g.transpose(1, 0, 2).reshape(TOKENS, KVH * HD)
    input_grad = jnp.dot(dquery, w_query.T, preferred_element_type=jnp.float32)
    input_grad = input_grad + jnp.dot(dkey, w_key.T, preferred_element_type=jnp.float32)
    input_grad = input_grad + jnp.dot(dvalue, w_value.T, preferred_element_type=jnp.float32)
    return (attention, input_grad.astype(jnp.bfloat16))
```

```python
import math

import jax
import jax.numpy as jnp
from jax import lax
from jax.experimental import pallas as pl
from jax.experimental.pallas import tpu as pltpu
from jax.sharding import PartitionSpec as P

HD = 128
QPK = 4
NEG = -1e30
SCALE = 1.0 / math.sqrt(HD)
LOG2E = 1.0 / math.log(2.0)
BF = jnp.bfloat16
F32 = jnp.float32
CHUNKS = 4
HALVES = 2


def dot_nt(a, b):
    return lax.dot_general(a, b, (((1,), (1,)), ((), ())), preferred_element_type=F32)


def dot_tn(a, b):
    return lax.dot_general(a, b, (((0,), (0,)), ((), ())), preferred_element_type=F32)


def dot_nn(a, b):
    return jnp.dot(a, b, preferred_element_type=F32)


def row_starts(len_ref, rank, rows):
    pos = rank * rows + lax.broadcasted_iota(jnp.int32, (rows, 1), 0)
    start = jnp.zeros((rows, 1), jnp.int32)
    end = 0
    for i in range(len_ref.shape[0]):
        end = end + len_ref[i]
        start = jnp.where(pos >= end, end, start)
    return start


def one_if(cond):
    return jnp.where(cond, 1.0, 0.0)


def arrivals(block_ref, rank, ranks):
    each = block_ref.shape[0] // ranks
    has = []
    for t in range(ranks):
        count = 0
        for k in range(each):
            count = count + jnp.where(block_ref[t * each + k] == rank, 1, 0)
        has.append(count)

    def place(target):
        return sum(jnp.where(t < target, has[t], 0) for t in range(ranks))

    return has, place


def bias_of(start, rank, keys):
    rows = start.shape[0]
    qpos = rank * rows + lax.broadcasted_iota(jnp.int32, (rows, keys), 0)
    col = lax.broadcasted_iota(jnp.int32, (rows, keys), 1)
    slot = col // rows
    kpos = (rank - 2 * slot) * rows + col
    seen = (kpos <= qpos) & (kpos >= start)
    return jnp.where(seen, 0.0, NEG)


def pick(source, block, wanted):
    total = None
    for b in range(source.shape[0] // block):
        term = source[b * block : (b + 1) * block, :].astype(F32) * wanted(b)
        total = term if total is None else total + term
    return total.astype(BF)


def attend_head(h, q_ref, kv_ref, g_ref, bias_ref, att_ref, dq_ref, dkv_ref, first):
    half = kv_ref.shape[1] // 2
    hs = slice(h * HD, (h + 1) * HD)
    g = h // QPK
    k = kv_ref[:, g * HD : (g + 1) * HD]
    v = kv_ref[:, half + g * HD : half + (g + 1) * HD]
    q = q_ref[:, hs]
    go = g_ref[:, hs]
    s = dot_nt(q, k) * (SCALE * LOG2E) + bias_ref[...]
    m = jnp.max(s, axis=1, keepdims=True)
    p = jnp.exp2(s - m)
    w = p * (1.0 / jnp.sum(p, axis=1, keepdims=True))
    wb = w.astype(BF)
    att = dot_nn(wb, v).astype(BF)
    att_ref[:, hs] = att
    delta = jnp.sum(go.astype(F32) * att.astype(F32), axis=1, keepdims=True)
    ds = (w * (dot_nt(go, v) - delta)).astype(BF)
    dq_ref[:, hs] = (dot_nn(ds, k) * SCALE).astype(BF)
    dk = dot_tn(ds, q)
    dv = dot_tn(wb, go)
    if first:
        dkv_ref[:, :HD] = dk
        dkv_ref[:, HD:] = dv
    else:
        dkv_ref[:, :HD] += dk
        dkv_ref[:, HD:] += dv


def kernel(
    block_ref, len_ref, x_hbm, grad_hbm, wq_hbm, wk_hbm, wv_hbm,
    att_ref, out_ref,
    xall, acc, slots, got, back, wq, wk, wv, kv, q, g, bias, att, dq, sums,
    send, xrx, zsend, zrx, dk, dv, near_tx, pre_tx, far_tx,
    wsem, xsem, gsem, ready,
    ns, nr, fs, fr, gs, gr, asend, arecv, zs, zr, xs, xr,
    bxs, bxr, bzs, bzr, bsend, brecv, ps, pr, f2s, f2r, n2s, n2r,
):
    rank = lax.axis_index("ctx")
    head = lax.axis_index("heads")
    ranks = lax.axis_size("ctx")
    nheads = lax.axis_size("heads")
    core = lax.rem(head, 2)
    turn = 1 - 2 * core
    sib = head + turn
    chips = nheads // 2
    chip = head // 2
    side = lax.rem(rank, 2)
    pair = rank // 2
    pairs = ranks // 2
    mate = rank + 1 - 2 * side
    rows = q.shape[0]
    part = rows // HALVES
    width = xall.shape[3]
    feat = CHUNKS * width
    reach = ranks // 4
    wide = q.shape[1]
    half = kv.shape[1] // 2
    groups = half // HD
    block = slots.shape[1]
    nblk = rows // block
    barrier = pltpu.get_barrier_semaphore()

    def to(ctx, h):
        return dict(device_id=(ctx, h), device_id_type=pl.DeviceIdType.MESH)

    def across(d):
        return lax.rem(chip + d, chips) * 2 + core

    def behind(d):
        return lax.rem(chip + chips - d, chips) * 2 + core

    def cut(a):
        return slice(a * part, (a + 1) * part)

    def cols(c):
        return pl.ds(pl.multiple_of(c * width, width), width)

    def piece(t, c):
        return pl.ds(pl.multiple_of(t * feat + c * width, width), width)

    def remote(src, dst, ssem, rsem, target):
        return pltpu.make_async_remote_copy(
            src_ref=src, dst_ref=dst, send_sem=ssem, recv_sem=rsem, **target
        )

    for o in range(1, ranks):
        pl.semaphore_signal(barrier, inc=1, **to(lax.rem(rank + o, ranks), head))
    for d in range(1, chips):
        pl.semaphore_signal(barrier, inc=1, **to(rank, across(d)))
    pl.semaphore_signal(barrier, inc=1, **to(rank, sib))

    def xload(c):
        return pltpu.make_async_copy(x_hbm.at[:, cols(c)], xall.at[head, c], xsem.at[c])

    gload = pltpu.make_async_copy(grad_hbm, att, gsem)
    order = [head, sib]
    for d in range(1, chips):
        order = order + [behind(d), behind(d) + turn]

    def loads(n):
        at = pl.ds(pl.multiple_of(order[n] * feat, feat), feat)
        return [
            pltpu.make_async_copy(s.at[at, :], t.at[at, :], wsem.at[n, i])
            for i, (s, t) in enumerate(((wq_hbm, wq), (wk_hbm, wk), (wv_hbm, wv)))
        ]

    gload.start()
    for c in range(CHUNKS):
        xload(c).start()
    for n in range(nheads):
        for load in loads(n):
            load.start()
    for d in range(1, reach + 1):
        @pl.when(pair < d)
        def _():
            kv[2 * d * rows : (2 * d + 1) * rows, :] = jnp.zeros((rows, 2 * half), BF)

    @pl.when(pair + 1 == pairs)
    def _():
        zrx[...] = jnp.zeros_like(zrx)

    for gi in range(groups):
        xrx[gi, 0] = jnp.zeros(xrx.shape[2:], BF)
        xrx[gi, reach + 1] = jnp.zeros(xrx.shape[2:], BF)
    acc[...] = jnp.zeros_like(acc)
    pl.semaphore_wait(barrier, ranks + chips - 1)

    def far(d, a, c):
        return remote(
            x_hbm.at[cut(a), cols(c)], xall.at[head, c, cut(a)],
            fs.at[d - 1, a, c], fr.at[d - 1, a, c], to(rank, across(d)),
        )

    def near(c):
        return remote(
            x_hbm.at[:, cols(c)], xall.at[head, c], ns.at[c], nr.at[c], to(rank, sib)
        )

    def give(d, a, c):
        return remote(
            xall.at[behind(d), c, cut(a)], xall.at[behind(d), c, cut(a)],
            gs.at[d - 1, a, c], gr.at[d - 1, a, c], to(rank, sib),
        )

    for d in range(1, chips):
        for c in range(CHUNKS):
            far(d, 0, c).start()
    for c in range(CHUNKS):
        near(c).start()

    def acopy(o):
        return remote(
            slots.at[o], got.at[rank], asend.at[o], arecv.at[o],
            to(lax.rem(rank + o, ranks), head),
        )

    has, place = arrivals(block_ref, rank, ranks)
    gload.wait()
    for o in range(ranks):
        spot = place(lax.rem(rank + o, ranks))
        value = pick(att, block, lambda b: one_if(spot == b))
        if o == 0:
            got[rank] = value
        else:
            slots[o] = value
            acopy(o).start()

    def add_kv(x, r, t, c):
        at = piece(t, c)
        acc[r, wide : wide + half] += dot_nn(x, wk[at, :])
        acc[r, wide + half : wide + 2 * half] += dot_nn(x, wv[at, :])

    def add_q(x, r, t, c):
        acc[r, :wide] += dot_nn(x, wq[piece(t, c), :])

    everyrow = slice(0, rows)
    for load in loads(0):
        load.wait()

    @pl.loop(0, CHUNKS)
    def _(c):
        xload(c).wait()
        add_kv(xall[head, c], everyrow, head, c)
        add_q(xall[head, c], everyrow, head, c)

    for load in loads(1):
        load.wait()

    @pl.loop(0, CHUNKS)
    def _(c):
        near(c).wait()
        add_kv(xall[sib, c], everyrow, sib, c)
        add_q(xall[sib, c], everyrow, sib, c)

    for n in range(2, nheads):
        for load in loads(n):
            load.wait()

    def place_of(j, a):
        return pl.ds(pl.multiple_of(j * rows + a * part, part), part)

    def zcopy(d, a):
        return remote(
            kv.at[place_of(2 * d - 2, a), :], kv.at[place_of(2 * d, a), :],
            zs.at[d - 1, a], zr.at[d - 1, a], to(rank + 2, head),
        )

    def xcopy(i, a):
        return remote(
            kv.at[place_of(2 * (i + side), a), :], kv.at[place_of(2 * i + 1, a), :],
            xs.at[i, a], xr.at[i, a], to(mate, head),
        )

    def kv_begin(a):
        kv[a * part : (a + 1) * part, :] = acc[cut(a), wide : wide + 2 * half].astype(BF)

        @pl.when(pair + 1 < pairs)
        def _():
            zcopy(1, a).start()

        @pl.when(side == 0)
        def _():
            xcopy(0, a).start()

    def kv_step(d, a):
        @pl.when(pair >= d)
        def _():
            zcopy(d, a).wait_recv()

        if d < reach:
            @pl.when((pair >= d) & (pair + 1 < pairs))
            def _():
                zcopy(d + 1, a).start()

            @pl.when(side == 0)
            def _():
                xcopy(d, a).start()

        @pl.when(side == 1)
        def _():
            xcopy(d - 1, a).start()

    def kv_end(a):
        for i in range(reach):
            xcopy(i, a).wait()
        for d in range(1, reach + 1):
            @pl.when((pair >= d - 1) & (pair + 1 < pairs))
            def _():
                zcopy(d, a).wait_send()

    last = CHUNKS - 1
    for a in range(HALVES):
        for d in range(1, chips):
            one = behind(d)
            two = one + turn

            @pl.loop(0, CHUNKS)
            def _(c):
                far(d, a, c).wait()
                give(d, a, c).start()
                if a + 1 < HALVES:
                    far(d, a + 1, c).start()
                add_kv(xall[one, c, cut(a)], cut(a), one, c)

                @pl.when(c > 0)
                def _():
                    add_q(xall[one, c - 1, cut(a)], cut(a), one, c - 1)
                    add_q(xall[two, c - 1, cut(a)], cut(a), two, c - 1)

                give(d, a, c).wait()
                add_kv(xall[two, c, cut(a)], cut(a), two, c)
                if a > 0 and d == chips - 1:
                    for e in range(1, reach + 1):
                        @pl.when(c == e * CHUNKS // reach - 1)
                        def _():
                            kv_step(e, a - 1)

            if d == chips - 1:
                kv_begin(a)
            add_q(xall[one, last, cut(a)], cut(a), one, last)
            add_q(xall[two, last, cut(a)], cut(a), two, last)

    for d in range(1, chips):
        pl.semaphore_signal(ready, inc=1, **to(rank, across(d)))
    pl.semaphore_signal(ready, inc=1, **to(rank, sib))
    q[...] = acc[:, :wide].astype(BF)
    kv_step(1, HALVES - 1)
    bias[...] = bias_of(row_starts(len_ref, rank, rows), rank, kv.shape[0])
    for o in range(1, ranks):
        acopy(o).wait()
    for b in range(nblk):
        target = block_ref[rank * nblk + b]
        total = jnp.zeros(slots.shape[1:], F32)
        for s in range(ranks):
            total = total + got[s].astype(F32) * one_if(target == s)
        g[b * block : (b + 1) * block, :] = total.astype(BF)
    for d in range(2, reach + 1):
        kv_step(d, HALVES - 1)
    for a in range(HALVES):
        kv_end(a)

    def bx(gi, i, a):
        return remote(
            send.at[gi, 2 * i + 1, cut(a)], xrx.at[gi, i + 1, cut(a)],
            bxs.at[gi, i, a], bxr.at[gi, i, a], to(mate, head),
        )

    def bz(gi, d, a):
        return remote(
            zsend.at[gi, d - 1, cut(a)], zrx.at[gi, d - 1, cut(a)],
            bzs.at[gi, d - 1, a], bzr.at[gi, d - 1, a], to(rank - 2, head),
        )

    def put_dkv(gi):
        send[gi, :, :, :HD] = (sums[:, :HD] * SCALE).astype(BF).reshape(send.shape[1:3] + (HD,))
        send[gi, :, :, HD:] = sums[:, HD:].astype(BF).reshape(send.shape[1:3] + (HD,))
        for a in range(HALVES):
            for i in reversed(range(reach)):
                bx(gi, i, a).start()

    def level(gi, d, a):
        if d == reach:
            for i in range(reach):
                bx(gi, i, a).wait()

        def whole():
            both = send[gi, 2 * d, cut(a)].astype(F32) + xrx[gi, d + 1 - side, cut(a)].astype(F32)
            if d < reach:
                both = both + zrx[gi, d, cut(a)].astype(F32)
            return both.astype(BF)

        if d < reach:
            @pl.when((pair >= d) & (pair + 1 < pairs))
            def _():
                bz(gi, d + 1, a).wait_recv()

        if d > 0:
            @pl.when(pair >= d)
            def _():
                zsend[gi, d - 1, cut(a)] = whole()
                bz(gi, d, a).start()
        else:
            total = whole()
            dk[cut(a), gi * HD : (gi + 1) * HD] = total[:, :HD]
            dv[cut(a), gi * HD : (gi + 1) * HD] = total[:, HD:]

    for gi in range(groups):
        for i in range(QPK):
            attend_head(gi * QPK + i, q, kv, g, bias, att, dq, sums, i == 0)
            if gi > 0 and i == 1:
                for a in range(HALVES):
                    level(gi - 1, reach, a)
            if gi > 0 and i == 2:
                for d in range(reach - 1, 0, -1):
                    for a in range(HALVES):
                        level(gi - 1, d, a)
        put_dkv(gi)
        if gi > 0:
            for a in range(HALVES):
                level(gi - 1, 0, a)

    def bcopy(o):
        return remote(
            slots.at[o], back.at[rank], bsend.at[o], brecv.at[o],
            to(lax.rem(rank + o, ranks), head),
        )

    for o in range(ranks):
        target = lax.rem(rank + o, ranks)
        value = pick(att, block, lambda b: one_if(block_ref[rank * nblk + b] == target))
        if o == 0:
            back[rank] = value
        else:
            slots[o] = value
    for d in range(reach, 0, -1):
        for a in range(HALVES):
            level(groups - 1, d, a)

    def term(t, c, r):
        at = piece(t, c)
        return dot_nt(dq[r, :], wq[at, :]) + dot_nt(dk[r, :], wk[at, :]) + dot_nt(dv[r, :], wv[at, :])

    def pre(d, a, c):
        return remote(
            pre_tx.at[d - 1, c, cut(a)], xall.at[behind(d), c, cut(a)],
            ps.at[d - 1, a, c], pr.at[d - 1, a, c], to(rank, sib),
        )

    def far2(d, a, c):
        return remote(
            far_tx.at[d - 1, c, cut(a)], xall.at[head, c, cut(a)],
            f2s.at[d - 1, a, c], f2r.at[d - 1, a, c], to(rank, across(d)),
        )

    def near2(c):
        return remote(near_tx.at[c], xall.at[head, c], n2s.at[c], n2r.at[c], to(rank, sib))

    pl.semaphore_wait(ready, chips)
    for a in range(HALVES):
        level(groups - 1, 0, a)
        if a == 0:
            for o in range(1, ranks):
                bcopy(o).start()

        for d in range(1, chips):
            @pl.loop(0, CHUNKS)
            def _(c):
                pre_tx[d - 1, c, cut(a)] = term(across(d) + turn, c, cut(a)).astype(BF)
                pre(d, a, c).start()
                mine = term(across(d), c, cut(a))
                pre(d, a, c).wait()
                mine = mine + xall[behind(d) + turn, c, cut(a)].astype(F32)
                far_tx[d - 1, c, cut(a)] = mine.astype(BF)
                far2(d, a, c).start()

    @pl.loop(0, CHUNKS)
    def _(c):
        near_tx[c] = term(sib, c, everyrow).astype(BF)
        near2(c).start()
        acc[:, cols(c)] = term(head, c, everyrow)

    for gi in range(groups):
        for d in range(1, reach + 1):
            for a in range(HALVES):
                @pl.when(pair >= d)
                def _():
                    bz(gi, d, a).wait_send()

    for o in range(1, ranks):
        bcopy(o).wait()
    spots = [place(t) for t in range(ranks)]
    for b in range(nblk):
        total = jnp.zeros(slots.shape[1:], F32)
        for t in range(ranks):
            total = total + back[t].astype(F32) * one_if((has[t] > 0) & (spots[t] == b))
        att_ref[b * block : (b + 1) * block, :] = total.astype(BF)
    for a in range(HALVES):
        @pl.loop(0, CHUNKS)
        def _(c):
            if a == 0:
                near2(c).wait()
            total = acc[cut(a), cols(c)] + xall[sib, c, cut(a)].astype(F32)
            for d in range(1, chips):
                far2(d, a, c).wait()
                total = total + xall[behind(d), c, cut(a)].astype(F32)
            out_ref[cut(a), cols(c)] = total.astype(BF)


def per_device(activations, w_query, w_key, w_value, doc_lengths, block_dest, out_grad):
    ranks = lax.axis_size("ctx")
    nheads = lax.axis_size("heads")
    chips = nheads // 2
    rows, feat = activations.shape
    block = rows * ranks // block_dest.shape[0]
    cw = feat // CHUNKS
    wide = w_query.shape[1]
    half = w_key.shape[1]
    groups = half // HD
    reach = ranks // 4
    slots = 2 * reach + 1
    keys = slots * rows
    vm = pl.BlockSpec(memory_space=pltpu.VMEM)
    hbm = pl.BlockSpec(memory_space=pl.ANY)
    dma = pltpu.SemaphoreType.DMA
    return pl.pallas_call(
        kernel,
        out_shape=(
            jax.ShapeDtypeStruct((rows, wide), BF),
            jax.ShapeDtypeStruct((rows, feat), BF),
        ),
        in_specs=[pl.BlockSpec(memory_space=pltpu.SMEM)] * 2 + [hbm] * 5,
        out_specs=(vm, vm),
        scratch_shapes=[
            pltpu.VMEM((nheads, CHUNKS, rows, cw), BF),
            pltpu.VMEM((rows, max(feat, wide + 2 * half)), F32),
            pltpu.VMEM((ranks, block, wide), BF),
            pltpu.VMEM((ranks, block, wide), BF),
            pltpu.VMEM((ranks, block, wide), BF),
            pltpu.VMEM(w_query.shape, BF),
            pltpu.VMEM(w_key.shape, BF),
            pltpu.VMEM(w_value.shape, BF),
            pltpu.VMEM((keys, 2 * half), BF),
            pltpu.VMEM((rows, wide), BF),
            pltpu.VMEM((rows, wide), BF),
            pltpu.VMEM((rows, keys), F32),
            pltpu.VMEM((rows, wide), BF),
            pltpu.VMEM((rows, wide), BF),
            pltpu.VMEM((keys, 2 * HD), F32),
            pltpu.VMEM((groups, slots, rows, 2 * HD), BF),
            pltpu.VMEM((groups, reach + 2, rows, 2 * HD), BF),
            pltpu.VMEM((groups, reach, rows, 2 * HD), BF),
            pltpu.VMEM((groups, reach, rows, 2 * HD), BF),
            pltpu.VMEM((rows, half), BF),
            pltpu.VMEM((rows, half), BF),
            pltpu.VMEM((CHUNKS, rows, cw), BF),
            pltpu.VMEM((chips - 1, CHUNKS, rows, cw), BF),
            pltpu.VMEM((chips - 1, CHUNKS, rows, cw), BF),
            dma((nheads, 3)),
            dma((CHUNKS,)),
            dma,
            pltpu.SemaphoreType.REGULAR,
            dma((CHUNKS,)),
            dma((CHUNKS,)),
            dma((chips - 1, HALVES, CHUNKS)),
            dma((chips - 1, HALVES, CHUNKS)),
            dma((chips - 1, HALVES, CHUNKS)),
            dma((chips - 1, HALVES, CHUNKS)),
            dma((ranks,)),
            dma((ranks,)),
            dma((reach, HALVES)),
            dma((reach, HALVES)),
            dma((reach, HALVES)),
            dma((reach, HALVES)),
            dma((groups, reach, HALVES)),
            dma((groups, reach, HALVES)),
            dma((groups, reach, HALVES)),
            dma((groups, reach, HALVES)),
            dma((ranks,)),
            dma((ranks,)),
            dma((chips - 1, HALVES, CHUNKS)),
            dma((chips - 1, HALVES, CHUNKS)),
            dma((chips - 1, HALVES, CHUNKS)),
            dma((chips - 1, HALVES, CHUNKS)),
            dma((CHUNKS,)),
            dma((CHUNKS,)),
        ],
        compiler_params=pltpu.CompilerParams(
            vmem_limit_bytes=62 * 2**20, collective_id=1, has_side_effects=True
        ),
        name="attention",
    )(block_dest, doc_lengths, activations, out_grad, w_query, w_key, w_value)


def solution(mesh):
    return jax.shard_map(
        per_device,
        mesh=mesh,
        in_specs=(
            P("ctx", "heads"),
            P(None, "heads"),
            P(None, "heads"),
            P(None, "heads"),
            P(),
            P(),
            P("ctx", "heads"),
        ),
        out_specs=(P("ctx", "heads"), P("ctx", "heads")),
        check_vma=False,
    )
```

```python
import math

import jax
import jax.numpy as jnp
from jax import lax
from jax.experimental import pallas as pl
from jax.experimental.pallas import tpu as pltpu
from jax.sharding import PartitionSpec as P

HD = 128
QPK = 4
NEG = -1e30
SCALE = 1.0 / math.sqrt(HD)
LOG2E = 1.0 / math.log(2.0)
BF = jnp.bfloat16
F32 = jnp.float32
CHUNKS = 4
HALVES = 2


def dot_nt(a, b):
    return lax.dot_general(a, b, (((1,), (1,)), ((), ())), preferred_element_type=F32)


def dot_tn(a, b):
    return lax.dot_general(a, b, (((0,), (0,)), ((), ())), preferred_element_type=F32)


def dot_nn(a, b):
    return jnp.dot(a, b, preferred_element_type=F32)


def row_starts(len_ref, rank, rows):
    pos = rank * rows + lax.broadcasted_iota(jnp.int32, (rows, 1), 0)
    start = jnp.zeros((rows, 1), jnp.int32)
    end = 0
    for i in range(len_ref.shape[0]):
        end = end + len_ref[i]
        start = jnp.where(pos >= end, end, start)
    return start


def one_if(cond):
    return jnp.where(cond, 1.0, 0.0)


def arrivals(block_ref, rank, ranks):
    each = block_ref.shape[0] // ranks
    has = []
    for t in range(ranks):
        count = 0
        for k in range(each):
            count = count + jnp.where(block_ref[t * each + k] == rank, 1, 0)
        has.append(count)

    def place(target):
        return sum(jnp.where(t < target, has[t], 0) for t in range(ranks))

    return has, place


def bias_of(start, rank, keys):
    rows = start.shape[0]
    part = rows // HALVES
    qpos = rank * rows + lax.broadcasted_iota(jnp.int32, (rows, keys), 0)
    col = lax.broadcasted_iota(jnp.int32, (rows, keys), 1)
    later = col // (keys // HALVES)
    slot = (col - later * (keys // HALVES)) // part
    kpos = (rank - slot) * rows + later * part + lax.rem(col, part)
    seen = (kpos <= qpos) & (kpos >= start)
    return jnp.where(seen, 0.0, NEG)


def pick(source, block, wanted):
    total = None
    for b in range(source.shape[0] // block):
        term = source[b * block : (b + 1) * block, :].astype(F32) * wanted(b)
        total = term if total is None else total + term
    return total.astype(BF)


def split(h, kv_ref):
    half = kv_ref.shape[1] // 2
    g = h // QPK
    ks = slice(g * HD, (g + 1) * HD)
    vs = slice(half + g * HD, half + (g + 1) * HD)
    return slice(h * HD, (h + 1) * HD), ks, vs


def score(h, keys, w_ref, q_ref, kv_ref, bias_ref):
    hs, ks, _ = split(h, kv_ref)
    s = dot_nt(q_ref[:, hs], kv_ref[keys, ks])
    w_ref[h, :, keys] = s * (SCALE * LOG2E) + bias_ref[:, keys]


def attend(h, w_ref, kv_ref, att_ref):
    hs, _, vs = split(h, kv_ref)
    s = w_ref[h]
    m = jnp.max(s, axis=1, keepdims=True)
    p = jnp.exp2(s - m)
    w = p * (1.0 / jnp.sum(p, axis=1, keepdims=True))
    w_ref[h] = w
    att_ref[:, hs] = dot_nn(w.astype(BF), kv_ref[:, vs]).astype(BF)


def attend_back(h, w_ref, q_ref, kv_ref, g_ref, att_ref, dkv_ref):
    hs, _, vs = split(h, kv_ref)
    go = g_ref[:, hs]
    delta = jnp.sum(go.astype(F32) * att_ref[:, hs].astype(F32), axis=1, keepdims=True)
    w = w_ref[h]
    dv = dot_tn(w.astype(BF), go)
    ds = w * (dot_nt(go, kv_ref[:, vs]) - delta)
    w_ref[h] = ds
    dk = dot_tn(ds.astype(BF), q_ref[:, hs])
    if h % QPK == 0:
        dkv_ref[:, :HD] = dk
        dkv_ref[:, HD:] = dv
    else:
        dkv_ref[:, :HD] += dk
        dkv_ref[:, HD:] += dv


def attend_query(h, w_ref, kv_ref, dq_ref):
    hs, ks, _ = split(h, kv_ref)
    dq_ref[:, hs] = (dot_nn(w_ref[h].astype(BF), kv_ref[:, ks]) * SCALE).astype(BF)


def kernel(
    block_ref, len_ref, x_hbm, grad_hbm, wq_hbm, wk_hbm, wv_hbm,
    att_hbm, out_hbm,
    xall, acc, slots, got, back, wq, wk, wv, kv, q, g, bias, att, dq, sums, weights,
    send, xrx, zsend, zrx, dk, dv, pre_tx, far_tx,
    wsem, xsem, gsem, asem, osem, ready,
    ns, nr, fs, fr, gs, gr, asend, arecv, zs, zr, xs, xr,
    bxs, bxr, bzs, bzr, bsend, brecv, ps, pr, f2s, f2r, n2s, n2r,
):
    rank = lax.axis_index("ctx")
    head = lax.axis_index("heads")
    ranks = lax.axis_size("ctx")
    nheads = lax.axis_size("heads")
    core = lax.rem(head, 2)
    turn = 1 - 2 * core
    sib = head + turn
    chips = nheads // 2
    chip = head // 2
    side = lax.rem(rank, 2)
    pair = rank // 2
    pairs = ranks // 2
    mate = rank + 1 - 2 * side
    rows = q.shape[0]
    part = rows // HALVES
    width = xall.shape[3]
    feat = CHUNKS * width
    reach = ranks // 4
    nslots = 2 * reach + 1
    early = (nslots + 1) * part
    wide = q.shape[1]
    half = kv.shape[1] // 2
    groups = half // HD
    block = slots.shape[1]
    nblk = rows // block
    barrier = pltpu.get_barrier_semaphore()

    def to(ctx, h):
        return dict(device_id=(ctx, h), device_id_type=pl.DeviceIdType.MESH)

    def across(d):
        return lax.rem(chip + d, chips) * 2 + core

    def behind(d):
        return lax.rem(chip + chips - d, chips) * 2 + core

    def cut(a):
        return slice(a * part, (a + 1) * part)

    def cols(c):
        return pl.ds(pl.multiple_of(c * width, width), width)

    def piece(t, c):
        return pl.ds(pl.multiple_of(t * feat + c * width, width), width)

    def place_of(j, a):
        return pl.ds(pl.multiple_of((a * nslots + j) * part, part), part)

    def remote(src, dst, ssem, rsem, target):
        return pltpu.make_async_remote_copy(
            src_ref=src, dst_ref=dst, send_sem=ssem, recv_sem=rsem, **target
        )

    for o in range(1, ranks):
        pl.semaphore_signal(barrier, inc=1, **to(lax.rem(rank + o, ranks), head))
    for d in range(1, chips):
        pl.semaphore_signal(barrier, inc=1, **to(rank, across(d)))
    pl.semaphore_signal(barrier, inc=1, **to(rank, sib))

    def xload(c):
        return pltpu.make_async_copy(x_hbm.at[:, cols(c)], xall.at[head, c], xsem.at[c])

    gload = pltpu.make_async_copy(grad_hbm, att, gsem)
    order = [head, sib]
    for d in range(1, chips):
        order = order + [behind(d), behind(d) + turn]

    def loads(n):
        at = pl.ds(pl.multiple_of(order[n] * feat, feat), feat)
        return [
            pltpu.make_async_copy(s.at[at, :], t.at[at, :], wsem.at[n, i])
            for i, (s, t) in enumerate(((wq_hbm, wq), (wk_hbm, wk), (wv_hbm, wv)))
        ]

    gload.start()
    for c in range(CHUNKS):
        xload(c).start()
    for n in range(nheads):
        for load in loads(n):
            load.start()
    for d in range(1, reach + 1):
        @pl.when(pair < d)
        def _():
            for a in range(HALVES):
                kv[place_of(2 * d, a), :] = jnp.zeros((part, 2 * half), BF)

    @pl.when(pair + 1 == pairs)
    def _():
        zrx[...] = jnp.zeros_like(zrx)

    for gi in range(groups):
        xrx[gi, 0] = jnp.zeros(xrx.shape[2:], BF)
        xrx[gi, reach + 1] = jnp.zeros(xrx.shape[2:], BF)
    acc[...] = jnp.zeros_like(acc)
    pl.semaphore_wait(barrier, ranks + chips - 1)

    def far(d, a, c):
        return remote(
            x_hbm.at[cut(a), cols(c)], xall.at[head, c, cut(a)],
            fs.at[d - 1, a, c], fr.at[d - 1, a, c], to(rank, across(d)),
        )

    def near(c):
        return remote(
            x_hbm.at[:, cols(c)], xall.at[head, c], ns.at[c], nr.at[c], to(rank, sib)
        )

    def give(d, a, c):
        return remote(
            xall.at[behind(d), c, cut(a)], xall.at[behind(d), c, cut(a)],
            gs.at[d - 1, a, c], gr.at[d - 1, a, c], to(rank, sib),
        )

    for d in range(1, chips):
        for c in range(CHUNKS):
            far(d, 0, c).start()
    for c in range(CHUNKS):
        near(c).start()

    def acopy(o):
        return remote(
            slots.at[o], got.at[rank], asend.at[o], arecv.at[o],
            to(lax.rem(rank + o, ranks), head),
        )

    def batch(o):
        if o % 4 == 2:
            return 2
        return 1 if o > ranks // 2 else 0

    def send_batch(n):
        for o in range(1, ranks):
            if batch(o) == n:
                acopy(o).start()

    has, place = arrivals(block_ref, rank, ranks)
    gload.wait()
    for o in range(ranks):
        spot = place(lax.rem(rank + o, ranks))
        value = pick(att, block, lambda b: one_if(spot == b))
        if o == 0:
            got[rank] = value
        else:
            slots[o] = value
            if batch(o) == 0:
                acopy(o).start()

    def add_kv(x, r, t, c):
        at = piece(t, c)
        acc[r, wide : wide + half] += dot_nn(x, wk[at, :])
        acc[r, wide + half : wide + 2 * half] += dot_nn(x, wv[at, :])

    def add_q(x, r, t, c):
        acc[r, :wide] += dot_nn(x, wq[piece(t, c), :])

    everyrow = slice(0, rows)
    for load in loads(0):
        load.wait()

    @pl.loop(0, CHUNKS)
    def _(c):
        xload(c).wait()
        add_kv(xall[head, c], everyrow, head, c)
        add_q(xall[head, c], everyrow, head, c)

    for load in loads(1):
        load.wait()

    @pl.loop(0, CHUNKS)
    def _(c):
        near(c).wait()
        add_kv(xall[sib, c], everyrow, sib, c)
        add_q(xall[sib, c], everyrow, sib, c)

    for n in range(2, nheads):
        for load in loads(n):
            load.wait()

    def zcopy(d, a):
        return remote(
            kv.at[place_of(2 * d - 2, a), :], kv.at[place_of(2 * d, a), :],
            zs.at[d - 1, a], zr.at[d - 1, a], to(rank + 2, head),
        )

    def xcopy(i, a):
        return remote(
            kv.at[place_of(2 * (i + side), a), :], kv.at[place_of(2 * i + 1, a), :],
            xs.at[i, a], xr.at[i, a], to(mate, head),
        )

    def kv_begin(a):
        kv[place_of(0, a), :] = acc[cut(a), wide : wide + 2 * half].astype(BF)

        @pl.when(pair + 1 < pairs)
        def _():
            zcopy(1, a).start()

        @pl.when(side == 0)
        def _():
            xcopy(0, a).start()

    def kv_step(d, a):
        @pl.when(pair >= d)
        def _():
            zcopy(d, a).wait_recv()

        if d < reach:
            @pl.when((pair >= d) & (pair + 1 < pairs))
            def _():
                zcopy(d + 1, a).start()

            @pl.when(side == 0)
            def _():
                xcopy(d, a).start()

        @pl.when(side == 1)
        def _():
            xcopy(d - 1, a).start()

    def kv_end(a):
        for i in range(reach):
            xcopy(i, a).wait()
        for d in range(1, reach + 1):
            @pl.when((pair >= d - 1) & (pair + 1 < pairs))
            def _():
                zcopy(d, a).wait_send()

    last = CHUNKS - 1
    for a in range(HALVES):
        for d in range(1, chips):
            one = behind(d)
            two = one + turn

            @pl.loop(0, CHUNKS)
            def _(c):
                far(d, a, c).wait()
                give(d, a, c).start()
                if a + 1 < HALVES:
                    far(d, a + 1, c).start()
                add_kv(xall[one, c, cut(a)], cut(a), one, c)

                @pl.when(c > 0)
                def _():
                    add_q(xall[one, c - 1, cut(a)], cut(a), one, c - 1)
                    add_q(xall[two, c - 1, cut(a)], cut(a), two, c - 1)

                give(d, a, c).wait()
                add_kv(xall[two, c, cut(a)], cut(a), two, c)
                if a > 0 and d == chips - 1:
                    for e in range(1, reach + 1):
                        @pl.when(c == e - 1)
                        def _():
                            kv_step(e, a - 1)

                    @pl.when(c == min(reach, last))
                    def _():
                        send_batch(1)

            if d == chips - 1:
                kv_begin(a)
            add_q(xall[one, last, cut(a)], cut(a), one, last)
            add_q(xall[two, last, cut(a)], cut(a), two, last)

    for d in range(1, chips):
        pl.semaphore_signal(ready, inc=1, **to(rank, across(d)))
    pl.semaphore_signal(ready, inc=1, **to(rank, sib))
    q[...] = acc[:, :wide].astype(BF)
    bias[...] = bias_of(row_starts(len_ref, rank, rows), rank, kv.shape[0])
    heads = range(groups * QPK)
    for a in range(HALVES - 1):
        kv_end(a)
    for h in heads:
        score(h, slice(0, early), weights, q, kv, bias)
        for d in range(1, reach + 1):
            if h == d * len(heads) // (2 * reach):
                kv_step(d, HALVES - 1)
    send_batch(2)
    kv_end(HALVES - 1)

    def assemble_grad():
        for o in range(1, ranks):
            acopy(o).wait()
        for b in range(nblk):
            target = block_ref[rank * nblk + b]
            total = jnp.zeros(slots.shape[1:], F32)
            for s in range(ranks):
                total = total + got[s].astype(F32) * one_if(target == s)
            g[b * block : (b + 1) * block, :] = total.astype(BF)

    def bx(gi, i, a):
        return remote(
            send.at[gi, a, 2 * i + 1], xrx.at[gi, i + 1, cut(a)],
            bxs.at[gi, i, a], bxr.at[gi, i, a], to(mate, head),
        )

    def bz(gi, d, a):
        return remote(
            zsend.at[gi, d - 1, cut(a)], zrx.at[gi, d - 1, cut(a)],
            bzs.at[gi, d - 1, a], bzr.at[gi, d - 1, a], to(rank - 2, head),
        )

    def dkv_begin(gi, a):
        for i in reversed(range(reach)):
            bx(gi, i, a).start()

    def put_dkv(gi):
        shape = send.shape[1:4] + (HD,)
        send[gi, :, :, :, :HD] = (sums[:, :HD] * SCALE).astype(BF).reshape(shape)
        send[gi, :, :, :, HD:] = sums[:, HD:].astype(BF).reshape(shape)
        dkv_begin(gi, 0)

    def level(gi, d, a):
        if d == reach:
            for i in range(reach):
                bx(gi, i, a).wait()

        def whole():
            both = send[gi, a, 2 * d].astype(F32) + xrx[gi, d + 1 - side, cut(a)].astype(F32)
            if d < reach:
                both = both + zrx[gi, d, cut(a)].astype(F32)
            return both.astype(BF)

        if d < reach:
            @pl.when((pair >= d) & (pair + 1 < pairs))
            def _():
                bz(gi, d + 1, a).wait_recv()

        if d > 0:
            @pl.when(pair >= d)
            def _():
                zsend[gi, d - 1, cut(a)] = whole()
                bz(gi, d, a).start()
        else:
            total = whole()
            dk[cut(a), gi * HD : (gi + 1) * HD] = total[:, :HD]
            dv[cut(a), gi * HD : (gi + 1) * HD] = total[:, HD:]

    def bcopy(o):
        return remote(
            slots.at[o], back.at[rank], bsend.at[o], brecv.at[o],
            to(lax.rem(rank + o, ranks), head),
        )

    def put_att(o):
        target = lax.rem(rank + o, ranks)
        value = pick(att, block, lambda b: one_if(block_ref[rank * nblk + b] == target))
        if o == 0:
            back[rank] = value
        else:
            slots[o] = value

    for h in heads:
        score(h, slice(early, kv.shape[0]), weights, q, kv, bias)
        attend(h, weights, kv, att)
    assemble_grad()
    for o in range(2, ranks, 2):
        put_att(o)
        bcopy(o).start()
    for gi in range(groups):
        for i in range(QPK):
            attend_back(gi * QPK + i, weights, q, kv, g, att, sums)
        put_dkv(gi)
    def parked(t, c):
        n = t * CHUNKS + c
        per = kv.shape[0] // width
        return n // per, pl.ds(pl.multiple_of(lax.rem(n, per) * width, width), width)

    def query_part(t):
        @pl.loop(0, CHUNKS)
        def _(c):
            n, at = parked(t, c)
            weights[n, :, at] = dot_nt(dq[...], wq[piece(t, c), :])

    def levels(d, a):
        for gi in range(groups):
            level(gi, d, a)

    for h in heads:
        attend_query(h, weights, kv, dq)
        if h % QPK == QPK - 1:
            level(h // QPK, reach, 0)
    for a in range(1, HALVES):
        for gi in range(groups):
            dkv_begin(gi, a)
    for d in range(1, chips):
        query_part(across(d) + turn)
    for d in range(reach - 1, 0, -1):
        levels(d, 0)
    for d in range(1, chips):
        query_part(across(d))
    put_att(0)
    for o in range(1, ranks, 2):
        put_att(o)
    levels(0, 0)

    def term(t, c, r):
        at = piece(t, c)
        n, spot = parked(t, c)
        return weights[n, r, spot] + dot_nt(dk[r, :], wk[at, :]) + dot_nt(dv[r, :], wv[at, :])

    def pre(d, a, c):
        return remote(
            pre_tx.at[d - 1, c, cut(a)], xall.at[behind(d), c, cut(a)],
            ps.at[d - 1, a, c], pr.at[d - 1, a, c], to(rank, sib),
        )

    def far2(d, a, c):
        return remote(
            far_tx.at[d - 1, c, cut(a)], xall.at[head, c, cut(a)],
            f2s.at[d - 1, a, c], f2r.at[d - 1, a, c], to(rank, across(d)),
        )

    def near2(c):
        return remote(xall.at[head, c], xall.at[head, c], n2s.at[c], n2r.at[c], to(rank, sib))

    def others(a):
        for d in range(1, chips):
            def forward(c):
                mine = term(across(d), c, cut(a))
                pre(d, a, c).wait()
                mine = mine + xall[behind(d) + turn, c, cut(a)].astype(F32)
                far_tx[d - 1, c, cut(a)] = mine.astype(BF)
                far2(d, a, c).start()

            @pl.loop(0, CHUNKS)
            def _(c):
                pre_tx[d - 1, c, cut(a)] = term(across(d) + turn, c, cut(a)).astype(BF)
                pre(d, a, c).start()

                @pl.when(c > 0)
                def _():
                    forward(c - 1)

            forward(last)

    pl.semaphore_wait(ready, chips)
    others(0)
    for a in range(1, HALVES):
        levels(reach, a)
        query_part(sib)
        for d in range(reach - 1, 0, -1):
            levels(d, a)
        query_part(head)
        for o in range(1, ranks, 2):
            bcopy(o).start()
        levels(0, a)
        others(a)

    @pl.loop(0, CHUNKS)
    def _(c):
        xall[head, c] = term(sib, c, everyrow).astype(BF)
        near2(c).start()
        acc[:, cols(c)] = term(head, c, everyrow)

    for gi in range(groups):
        for d in range(1, reach + 1):
            for a in range(HALVES):
                @pl.when(pair >= d)
                def _():
                    bz(gi, d, a).wait_send()

    for o in range(1, ranks):
        bcopy(o).wait()
    spots = [place(t) for t in range(ranks)]
    for b in range(nblk):
        total = jnp.zeros(slots.shape[1:], F32)
        for t in range(ranks):
            total = total + back[t].astype(F32) * one_if((has[t] > 0) & (spots[t] == b))
        att[b * block : (b + 1) * block, :] = total.astype(BF)
    astore = pltpu.make_async_copy(att, att_hbm, asem)
    astore.start()

    def store(a, c):
        return pltpu.make_async_copy(
            far_tx.at[0, c, cut(a)], out_hbm.at[cut(a), cols(c)], osem.at[a, c]
        )

    for a in range(HALVES):
        @pl.loop(0, CHUNKS)
        def _(c):
            if a == 0:
                near2(c).wait()
            total = acc[cut(a), cols(c)] + xall[sib, c, cut(a)].astype(F32)
            for d in range(1, chips):
                far2(d, a, c).wait()
                total = total + xall[behind(d), c, cut(a)].astype(F32)
            far_tx[0, c, cut(a)] = total.astype(BF)
            store(a, c).start()

    astore.wait()
    for a in range(HALVES):
        for c in range(CHUNKS):
            store(a, c).wait()


def finish_kernel(att_in, out_in, att_hbm, out_hbm, att, out, isem, osem):
    rows = out_in.shape[0] // CHUNKS
    copies = [(att_in, att, att_hbm)]
    for i in range(CHUNKS):
        at = pl.ds(i * rows, rows)
        copies.append((out_in.at[at], out.at[at], out_hbm.at[at]))
    inward = [pltpu.make_async_copy(c[0], c[1], isem.at[i]) for i, c in enumerate(copies)]
    outward = [pltpu.make_async_copy(c[1], c[2], osem.at[i]) for i, c in enumerate(copies)]
    for copy in inward:
        copy.start()
    for one, two in zip(inward, outward):
        one.wait()
        two.start()
    for copy in outward:
        copy.wait()


def finish(att, out):
    hbm = pl.BlockSpec(memory_space=pl.ANY)
    dma = pltpu.SemaphoreType.DMA
    return pl.pallas_call(
        finish_kernel,
        out_shape=tuple(jax.ShapeDtypeStruct(x.shape, x.dtype) for x in (att, out)),
        in_specs=[hbm] * 2,
        out_specs=(hbm,) * 2,
        scratch_shapes=[
            pltpu.VMEM(att.shape, BF),
            pltpu.VMEM(out.shape, BF),
            dma((CHUNKS + 1,)),
            dma((CHUNKS + 1,)),
        ],
        name="finish",
    )(att, out)


def per_device(activations, w_query, w_key, w_value, doc_lengths, block_dest, out_grad):
    ranks = lax.axis_size("ctx")
    nheads = lax.axis_size("heads")
    chips = nheads // 2
    rows, feat = activations.shape
    block = rows * ranks // block_dest.shape[0]
    cw = feat // CHUNKS
    wide = w_query.shape[1]
    half = w_key.shape[1]
    groups = half // HD
    reach = ranks // 4
    slots = 2 * reach + 1
    keys = slots * rows
    hbm = pl.BlockSpec(memory_space=pl.ANY)
    dma = pltpu.SemaphoreType.DMA
    att, out = pl.pallas_call(
        kernel,
        out_shape=(
            jax.ShapeDtypeStruct((rows, wide), BF),
            jax.ShapeDtypeStruct((rows, feat), BF),
        ),
        in_specs=[pl.BlockSpec(memory_space=pltpu.SMEM)] * 2 + [hbm] * 5,
        out_specs=(hbm, hbm),
        scratch_shapes=[
            pltpu.VMEM((nheads, CHUNKS, rows, cw), BF),
            pltpu.VMEM((rows, max(feat, wide + 2 * half)), F32),
            pltpu.VMEM((ranks, block, wide), BF),
            pltpu.VMEM((ranks, block, wide), BF),
            pltpu.VMEM((ranks, block, wide), BF),
            pltpu.VMEM(w_query.shape, BF),
            pltpu.VMEM(w_key.shape, BF),
            pltpu.VMEM(w_value.shape, BF),
            pltpu.VMEM((keys, 2 * half), BF),
            pltpu.VMEM((rows, wide), BF),
            pltpu.VMEM((rows, wide), BF),
            pltpu.VMEM((rows, keys), F32),
            pltpu.VMEM((rows, wide), BF),
            pltpu.VMEM((rows, wide), BF),
            pltpu.VMEM((keys, 2 * HD), F32),
            pltpu.VMEM((groups * QPK, rows, keys), F32),
            pltpu.VMEM((groups, HALVES, slots, rows // HALVES, 2 * HD), BF),
            pltpu.VMEM((groups, reach + 2, rows, 2 * HD), BF),
            pltpu.VMEM((groups, reach, rows, 2 * HD), BF),
            pltpu.VMEM((groups, reach, rows, 2 * HD), BF),
            pltpu.VMEM((rows, half), BF),
            pltpu.VMEM((rows, half), BF),
            pltpu.VMEM((chips - 1, CHUNKS, rows, cw), BF),
            pltpu.VMEM((chips - 1, CHUNKS, rows, cw), BF),
            dma((nheads, 3)),
            dma((CHUNKS,)),
            dma,
            dma,
            dma((HALVES, CHUNKS)),
            pltpu.SemaphoreType.REGULAR,
            dma((CHUNKS,)),
            dma((CHUNKS,)),
            dma((chips - 1, HALVES, CHUNKS)),
            dma((chips - 1, HALVES, CHUNKS)),
            dma((chips - 1, HALVES, CHUNKS)),
            dma((chips - 1, HALVES, CHUNKS)),
            dma((ranks,)),
            dma((ranks,)),
            dma((reach, HALVES)),
            dma((reach, HALVES)),
            dma((reach, HALVES)),
            dma((reach, HALVES)),
            dma((groups, reach, HALVES)),
            dma((groups, reach, HALVES)),
            dma((groups, reach, HALVES)),
            dma((groups, reach, HALVES)),
            dma((ranks,)),
            dma((ranks,)),
            dma((chips - 1, HALVES, CHUNKS)),
            dma((chips - 1, HALVES, CHUNKS)),
            dma((chips - 1, HALVES, CHUNKS)),
            dma((chips - 1, HALVES, CHUNKS)),
            dma((CHUNKS,)),
            dma((CHUNKS,)),
        ],
        compiler_params=pltpu.CompilerParams(
            vmem_limit_bytes=62 * 2**20, collective_id=1, has_side_effects=True
        ),
        name="attention",
    )(block_dest, doc_lengths, activations, out_grad, w_query, w_key, w_value)
    return finish(att, out)


def solution(mesh):
    return jax.shard_map(
        per_device,
        mesh=mesh,
        in_specs=(
            P("ctx", "heads"),
            P(None, "heads"),
            P(None, "heads"),
            P(None, "heads"),
            P(),
            P(),
            P("ctx", "heads"),
        ),
        out_specs=(P("ctx", "heads"), P("ctx", "heads")),
        check_vma=False,
    )
```

```python
import math

import jax
import jax.numpy as jnp
from jax import lax
from jax.experimental import pallas as pl
from jax.experimental.pallas import tpu as pltpu
from jax.sharding import PartitionSpec as P

HD = 128
QPK = 4
NEG = -1e30
SCALE = 1.0 / math.sqrt(HD)
LOG2E = 1.0 / math.log(2.0)
BF = jnp.bfloat16
F32 = jnp.float32
CHUNKS = 4
HALVES = 2


def dot_nt(a, b):
    return lax.dot_general(a, b, (((1,), (1,)), ((), ())), preferred_element_type=F32)


def dot_tn(a, b):
    return lax.dot_general(a, b, (((0,), (0,)), ((), ())), preferred_element_type=F32)


def dot_nn(a, b):
    return jnp.dot(a, b, preferred_element_type=F32)


def row_starts(len_ref, rank, rows):
    pos = rank * rows + lax.broadcasted_iota(jnp.int32, (rows, 1), 0)
    start = jnp.zeros((rows, 1), jnp.int32)
    end = 0
    for i in range(len_ref.shape[0]):
        end = end + len_ref[i]
        start = jnp.where(pos >= end, end, start)
    return start


def one_if(cond):
    return jnp.where(cond, 1.0, 0.0)


def arrivals(block_ref, rank, ranks):
    each = block_ref.shape[0] // ranks
    has = []
    for t in range(ranks):
        count = 0
        for k in range(each):
            count = count + jnp.where(block_ref[t * each + k] == rank, 1, 0)
        has.append(count)

    def place(target):
        return sum(jnp.where(t < target, has[t], 0) for t in range(ranks))

    return has, place


def bias_of(start, rank, keys):
    rows = start.shape[0]
    part = rows // HALVES
    qpos = rank * rows + lax.broadcasted_iota(jnp.int32, (rows, keys), 0)
    col = lax.broadcasted_iota(jnp.int32, (rows, keys), 1)
    later = col // (keys // HALVES)
    slot = (col - later * (keys // HALVES)) // part
    kpos = (rank - slot) * rows + later * part + lax.rem(col, part)
    seen = (kpos <= qpos) & (kpos >= start)
    return jnp.where(seen, 0.0, NEG)


def pick(source, block, wanted):
    total = None
    for b in range(source.shape[0] // block):
        term = source[b * block : (b + 1) * block, :].astype(F32) * wanted(b)
        total = term if total is None else total + term
    return total.astype(BF)


def split(h, kv_ref):
    half = kv_ref.shape[1] // 2
    g = h // QPK
    ks = slice(g * HD, (g + 1) * HD)
    vs = slice(half + g * HD, half + (g + 1) * HD)
    return slice(h * HD, (h + 1) * HD), ks, vs


def score(h, keys, w_ref, q_ref, kv_ref, bias_ref):
    hs, ks, _ = split(h, kv_ref)
    s = dot_nt(q_ref[:, hs], kv_ref[keys, ks])
    w_ref[h, :, keys] = s * (SCALE * LOG2E) + bias_ref[:, keys]


def attend(h, w_ref, kv_ref, att_ref):
    hs, _, vs = split(h, kv_ref)
    s = w_ref[h]
    m = jnp.max(s, axis=1, keepdims=True)
    p = jnp.exp2(s - m)
    w = p * (1.0 / jnp.sum(p, axis=1, keepdims=True))
    w_ref[h] = w
    att_ref[:, hs] = dot_nn(w.astype(BF), kv_ref[:, vs]).astype(BF)


def attend_back(h, w_ref, q_ref, kv_ref, g_ref, att_ref, dkv_ref):
    hs, _, vs = split(h, kv_ref)
    go = g_ref[:, hs]
    delta = jnp.sum(go.astype(F32) * att_ref[:, hs].astype(F32), axis=1, keepdims=True)
    w = w_ref[h]
    dv = dot_tn(w.astype(BF), go)
    ds = w * (dot_nt(go, kv_ref[:, vs]) - delta)
    w_ref[h] = ds
    dk = dot_tn(ds.astype(BF), q_ref[:, hs])
    if h % QPK == 0:
        dkv_ref[:, :HD] = dk
        dkv_ref[:, HD:] = dv
    else:
        dkv_ref[:, :HD] += dk
        dkv_ref[:, HD:] += dv


def attend_query(h, w_ref, kv_ref, dq_ref):
    hs, ks, _ = split(h, kv_ref)
    dq_ref[:, hs] = (dot_nn(w_ref[h].astype(BF), kv_ref[:, ks]) * SCALE).astype(BF)


def kernel(
    block_ref, len_ref, x_hbm, grad_hbm, wq_hbm, wk_hbm, wv_hbm,
    att_hbm, out_hbm,
    xall, acc, slots, outgo, got, back, wq, wk, wv, kv, q, g, bias, att, dq, sums, weights,
    send, xrx, zsend, zrx, dk, dv, pre_tx, far_tx,
    wsem, xsem, gsem, asem, osem, ready,
    ns, nr, fs, fr, gs, gr, asend, arecv, zs, zr, xs, xr,
    bxs, bxr, bzs, bzr, bsend, brecv, ps, pr, f2s, f2r, n2s, n2r,
):
    rank = lax.axis_index("ctx")
    head = lax.axis_index("heads")
    ranks = lax.axis_size("ctx")
    nheads = lax.axis_size("heads")
    core = lax.rem(head, 2)
    turn = 1 - 2 * core
    sib = head + turn
    chips = nheads // 2
    chip = head // 2
    side = lax.rem(rank, 2)
    pair = rank // 2
    pairs = ranks // 2
    mate = rank + 1 - 2 * side
    rows = q.shape[0]
    part = rows // HALVES
    width = xall.shape[3]
    feat = CHUNKS * width
    reach = ranks // 4
    nslots = 2 * reach + 1
    early = (nslots + 1) * part
    wide = q.shape[1]
    half = kv.shape[1] // 2
    groups = half // HD
    block = slots.shape[1]
    nblk = rows // block
    barrier = pltpu.get_barrier_semaphore()

    def to(ctx, h):
        return dict(device_id=(ctx, h), device_id_type=pl.DeviceIdType.MESH)

    def across(d):
        return lax.rem(chip + d, chips) * 2 + core

    def behind(d):
        return lax.rem(chip + chips - d, chips) * 2 + core

    def cut(a):
        return slice(a * part, (a + 1) * part)

    def cols(c):
        return pl.ds(pl.multiple_of(c * width, width), width)

    def piece(t, c):
        return pl.ds(pl.multiple_of(t * feat + c * width, width), width)

    def place_of(j, a):
        return pl.ds(pl.multiple_of((a * nslots + j) * part, part), part)

    def remote(src, dst, ssem, rsem, target):
        return pltpu.make_async_remote_copy(
            src_ref=src, dst_ref=dst, send_sem=ssem, recv_sem=rsem, **target
        )

    for o in range(1, ranks):
        pl.semaphore_signal(barrier, inc=1, **to(lax.rem(rank + o, ranks), head))
    for d in range(1, chips):
        pl.semaphore_signal(barrier, inc=1, **to(rank, across(d)))
    pl.semaphore_signal(barrier, inc=1, **to(rank, sib))

    def xload(c):
        return pltpu.make_async_copy(x_hbm.at[:, cols(c)], xall.at[head, c], xsem.at[c])

    gload = pltpu.make_async_copy(grad_hbm, att, gsem)
    order = [head, sib]
    for d in range(1, chips):
        order = order + [behind(d), behind(d) + turn]

    def loads(n):
        at = pl.ds(pl.multiple_of(order[n] * feat, feat), feat)
        return [
            pltpu.make_async_copy(s.at[at, :], t.at[at, :], wsem.at[n, i])
            for i, (s, t) in enumerate(((wq_hbm, wq), (wk_hbm, wk), (wv_hbm, wv)))
        ]

    gload.start()
    for c in range(CHUNKS):
        xload(c).start()
    for n in range(nheads):
        for load in loads(n):
            load.start()
    for d in range(1, reach + 1):
        @pl.when(pair < d)
        def _():
            for a in range(HALVES):
                kv[place_of(2 * d, a), :] = jnp.zeros((part, 2 * half), BF)

    @pl.when(pair + 1 == pairs)
    def _():
        zrx[...] = jnp.zeros_like(zrx)

    for gi in range(groups):
        xrx[gi, 0] = jnp.zeros(xrx.shape[2:], BF)
        xrx[gi, reach + 1] = jnp.zeros(xrx.shape[2:], BF)
    acc[...] = jnp.zeros_like(acc)
    pl.semaphore_wait(barrier, ranks + chips - 1)

    def far(d, a, c):
        return remote(
            x_hbm.at[cut(a), cols(c)], xall.at[head, c, cut(a)],
            fs.at[d - 1, a, c], fr.at[d - 1, a, c], to(rank, across(d)),
        )

    def near(c):
        return remote(
            x_hbm.at[:, cols(c)], xall.at[head, c], ns.at[c], nr.at[c], to(rank, sib)
        )

    def give(d, a, c):
        return remote(
            xall.at[behind(d), c, cut(a)], xall.at[behind(d), c, cut(a)],
            gs.at[d - 1, a, c], gr.at[d - 1, a, c], to(rank, sib),
        )

    for d in range(1, chips):
        for c in range(CHUNKS):
            far(d, 0, c).start()
    for c in range(CHUNKS):
        near(c).start()

    def acopy(o):
        return remote(
            slots.at[o], got.at[rank], asend.at[o], arecv.at[o],
            to(lax.rem(rank + o, ranks), head),
        )

    def batch(o):
        if o % 4 == 2:
            return 2
        return 0

    def send_batch(n):
        for o in range(1, ranks):
            if batch(o) == n:
                acopy(o).start()

    has, place = arrivals(block_ref, rank, ranks)
    gload.wait()
    for o in range(ranks):
        spot = place(lax.rem(rank + o, ranks))
        value = pick(att, block, lambda b: one_if(spot == b))
        if o == 0:
            got[rank] = value
        else:
            slots[o] = value
            if batch(o) == 0:
                acopy(o).start()

    def add_kv(x, r, t, c):
        at = piece(t, c)
        acc[r, wide : wide + half] += dot_nn(x, wk[at, :])
        acc[r, wide + half : wide + 2 * half] += dot_nn(x, wv[at, :])

    def add_q(x, r, t, c):
        acc[r, :wide] += dot_nn(x, wq[piece(t, c), :])

    everyrow = slice(0, rows)
    for load in loads(0):
        load.wait()

    @pl.loop(0, CHUNKS)
    def _(c):
        xload(c).wait()
        add_kv(xall[head, c], everyrow, head, c)
        add_q(xall[head, c], everyrow, head, c)

    for load in loads(1):
        load.wait()

    @pl.loop(0, CHUNKS)
    def _(c):
        near(c).wait()
        add_kv(xall[sib, c], everyrow, sib, c)
        add_q(xall[sib, c], everyrow, sib, c)

    for n in range(2, nheads):
        for load in loads(n):
            load.wait()

    def zcopy(d, a):
        return remote(
            kv.at[place_of(2 * d - 2, a), :], kv.at[place_of(2 * d, a), :],
            zs.at[d - 1, a], zr.at[d - 1, a], to(rank + 2, head),
        )

    def xcopy(i, a):
        return remote(
            kv.at[place_of(2 * (i + side), a), :], kv.at[place_of(2 * i + 1, a), :],
            xs.at[i, a], xr.at[i, a], to(mate, head),
        )

    def kv_begin(a):
        kv[place_of(0, a), :] = acc[cut(a), wide : wide + 2 * half].astype(BF)

        @pl.when(pair + 1 < pairs)
        def _():
            zcopy(1, a).start()

        @pl.when(side == 0)
        def _():
            xcopy(0, a).start()

    def kv_step(d, a):
        @pl.when(pair >= d)
        def _():
            zcopy(d, a).wait_recv()

        if d < reach:
            @pl.when((pair >= d) & (pair + 1 < pairs))
            def _():
                zcopy(d + 1, a).start()

            @pl.when(side == 0)
            def _():
                xcopy(d, a).start()

        @pl.when(side == 1)
        def _():
            xcopy(d - 1, a).start()

    def kv_end(a):
        for i in range(reach):
            xcopy(i, a).wait()
        for d in range(1, reach + 1):
            @pl.when((pair >= d - 1) & (pair + 1 < pairs))
            def _():
                zcopy(d, a).wait_send()

    last = CHUNKS - 1
    for a in range(HALVES):
        for d in range(1, chips):
            one = behind(d)
            two = one + turn

            @pl.loop(0, CHUNKS)
            def _(c):
                far(d, a, c).wait()
                give(d, a, c).start()
                if a + 1 < HALVES:
                    far(d, a + 1, c).start()
                add_kv(xall[one, c, cut(a)], cut(a), one, c)

                @pl.when(c > 0)
                def _():
                    add_q(xall[one, c - 1, cut(a)], cut(a), one, c - 1)
                    add_q(xall[two, c - 1, cut(a)], cut(a), two, c - 1)

                give(d, a, c).wait()
                add_kv(xall[two, c, cut(a)], cut(a), two, c)
                if a > 0 and d == chips - 1:
                    for e in range(1, reach + 1):
                        @pl.when(c == e - 1)
                        def _():
                            kv_step(e, a - 1)

                    @pl.when(c == min(reach, last))
                    def _():
                        send_batch(1)

            if d == chips - 1:
                kv_begin(a)
            add_q(xall[one, last, cut(a)], cut(a), one, last)
            add_q(xall[two, last, cut(a)], cut(a), two, last)

    for d in range(1, chips):
        pl.semaphore_signal(ready, inc=1, **to(rank, across(d)))
    pl.semaphore_signal(ready, inc=1, **to(rank, sib))
    q[...] = acc[:, :wide].astype(BF)
    bias[...] = bias_of(row_starts(len_ref, rank, rows), rank, kv.shape[0])
    heads = range(groups * QPK)
    for a in range(HALVES - 1):
        kv_end(a)
    for h in heads:
        score(h, slice(0, early), weights, q, kv, bias)
        for d in range(1, reach + 1):
            if h == d * len(heads) // (2 * reach):
                kv_step(d, HALVES - 1)
    send_batch(2)
    kv_end(HALVES - 1)

    def assemble_grad():
        for o in range(1, ranks):
            acopy(o).wait()
        for b in range(nblk):
            target = block_ref[rank * nblk + b]
            total = jnp.zeros(slots.shape[1:], F32)
            for s in range(ranks):
                total = total + got[s].astype(F32) * one_if(target == s)
            g[b * block : (b + 1) * block, :] = total.astype(BF)

    def bx(gi, i, a):
        return remote(
            send.at[gi, a, 2 * i + 1], xrx.at[gi, i + 1, cut(a)],
            bxs.at[gi, i, a], bxr.at[gi, i, a], to(mate, head),
        )

    def bz(gi, d, a):
        return remote(
            zsend.at[gi, d - 1, cut(a)], zrx.at[gi, d - 1, cut(a)],
            bzs.at[gi, d - 1, a], bzr.at[gi, d - 1, a], to(rank - 2, head),
        )

    def dkv_begin(gi, a):
        for i in reversed(range(reach)):
            bx(gi, i, a).start()

    def put_dkv(gi):
        shape = send.shape[1:4] + (HD,)
        send[gi, :, :, :, :HD] = (sums[:, :HD] * SCALE).astype(BF).reshape(shape)
        send[gi, :, :, :, HD:] = sums[:, HD:].astype(BF).reshape(shape)
        dkv_begin(gi, 0)

    def level(gi, d, a):
        if d > 0:
            bx(gi, d - 1, a).wait()

        def whole():
            both = send[gi, a, 2 * d].astype(F32) + xrx[gi, d + 1 - side, cut(a)].astype(F32)
            if d < reach:
                both = both + zrx[gi, d, cut(a)].astype(F32)
            return both.astype(BF)

        if d < reach:
            @pl.when((pair >= d) & (pair + 1 < pairs))
            def _():
                bz(gi, d + 1, a).wait_recv()

        if d > 0:
            @pl.when(pair >= d)
            def _():
                zsend[gi, d - 1, cut(a)] = whole()
                bz(gi, d, a).start()
        else:
            total = whole()
            dk[cut(a), gi * HD : (gi + 1) * HD] = total[:, :HD]
            dv[cut(a), gi * HD : (gi + 1) * HD] = total[:, HD:]

    def bcopy(o):
        return remote(
            outgo.at[o], back.at[rank], bsend.at[o], brecv.at[o],
            to(lax.rem(rank + o, ranks), head),
        )

    def put_att(o):
        target = lax.rem(rank + o, ranks)
        value = pick(att, block, lambda b: one_if(block_ref[rank * nblk + b] == target))
        if o == 0:
            back[rank] = value
        else:
            outgo[o] = value

    for h in heads:
        score(h, slice(early, kv.shape[0]), weights, q, kv, bias)
        attend(h, weights, kv, att)
    for o in range(2, ranks, 2):
        put_att(o)
        bcopy(o).start()
    assemble_grad()
    for gi in range(groups):
        for i in range(QPK):
            attend_back(gi * QPK + i, weights, q, kv, g, att, sums)
        put_dkv(gi)
    def parked(t, c):
        n = t * CHUNKS + c
        per = kv.shape[0] // width
        return n // per, pl.ds(pl.multiple_of(lax.rem(n, per) * width, width), width)

    def query_part(t):
        @pl.loop(0, CHUNKS)
        def _(c):
            n, at = parked(t, c)
            weights[n, :, at] = dot_nt(dq[...], wq[piece(t, c), :])

    def levels(d, a):
        for gi in range(groups):
            level(gi, d, a)

    for h in heads:
        attend_query(h, weights, kv, dq)
        if h % QPK == QPK - 1:
            level(h // QPK, reach, 0)
    for a in range(1, HALVES):
        for gi in range(groups):
            dkv_begin(gi, a)
    for d in range(1, chips):
        query_part(across(d) + turn)
    for d in range(reach - 1, 0, -1):
        levels(d, 0)
    for d in range(1, chips):
        query_part(across(d))
    put_att(0)
    for o in range(1, ranks, 2):
        put_att(o)
    levels(0, 0)

    def term(t, c, r):
        at = piece(t, c)
        n, spot = parked(t, c)
        return weights[n, r, spot] + dot_nt(dk[r, :], wk[at, :]) + dot_nt(dv[r, :], wv[at, :])

    def pre(d, a, c):
        return remote(
            pre_tx.at[d - 1, c, cut(a)], xall.at[behind(d), c, cut(a)],
            ps.at[d - 1, a, c], pr.at[d - 1, a, c], to(rank, sib),
        )

    def far2(d, a, c):
        return remote(
            far_tx.at[d - 1, c, cut(a)], xall.at[head, c, cut(a)],
            f2s.at[d - 1, a, c], f2r.at[d - 1, a, c], to(rank, across(d)),
        )

    def near2(c):
        return remote(xall.at[head, c], xall.at[head, c], n2s.at[c], n2r.at[c], to(rank, sib))

    def others(a):
        for d in range(1, chips):
            def forward(c):
                mine = term(across(d), c, cut(a))
                pre(d, a, c).wait()
                mine = mine + xall[behind(d) + turn, c, cut(a)].astype(F32)
                far_tx[d - 1, c, cut(a)] = mine.astype(BF)
                far2(d, a, c).start()

            @pl.loop(0, CHUNKS)
            def _(c):
                pre_tx[d - 1, c, cut(a)] = term(across(d) + turn, c, cut(a)).astype(BF)
                pre(d, a, c).start()

                @pl.when(c > 0)
                def _():
                    forward(c - 1)

            forward(last)

    pl.semaphore_wait(ready, chips)
    others(0)
    for a in range(1, HALVES):
        levels(reach, a)
        query_part(sib)
        for d in range(reach - 1, 0, -1):
            levels(d, a)
        query_part(head)
        for o in range(1, ranks, 2):
            bcopy(o).start()
        levels(0, a)
        others(a)

    @pl.loop(0, CHUNKS)
    def _(c):
        xall[head, c] = term(sib, c, everyrow).astype(BF)
        near2(c).start()
        acc[:, cols(c)] = term(head, c, everyrow)

    for gi in range(groups):
        for d in range(1, reach + 1):
            for a in range(HALVES):
                @pl.when(pair >= d)
                def _():
                    bz(gi, d, a).wait_send()

    def store(a, c):
        return pltpu.make_async_copy(
            far_tx.at[0, c, cut(a)], out_hbm.at[cut(a), cols(c)], osem.at[a, c]
        )

    def finish_rows(a):
        @pl.loop(0, CHUNKS)
        def _(c):
            if a == 0:
                near2(c).wait()
            total = acc[cut(a), cols(c)] + xall[sib, c, cut(a)].astype(F32)
            for d in range(1, chips):
                far2(d, a, c).wait()
                total = total + xall[behind(d), c, cut(a)].astype(F32)
            far_tx[0, c, cut(a)] = total.astype(BF)
            store(a, c).start()

    for a in range(HALVES - 1):
        finish_rows(a)
    for o in range(1, ranks):
        bcopy(o).wait()
    spots = [place(t) for t in range(ranks)]
    for b in range(nblk):
        total = jnp.zeros(slots.shape[1:], F32)
        for t in range(ranks):
            total = total + back[t].astype(F32) * one_if((has[t] > 0) & (spots[t] == b))
        att[b * block : (b + 1) * block, :] = total.astype(BF)
    astore = pltpu.make_async_copy(att, att_hbm, asem)
    astore.start()
    finish_rows(HALVES - 1)
    astore.wait()
    for a in range(HALVES):
        for c in range(CHUNKS):
            store(a, c).wait()


def finish_kernel(att_in, out_in, att_hbm, out_hbm, att, out, isem, osem):
    rows = out_in.shape[0] // CHUNKS
    copies = [(att_in, att, att_hbm)]
    for i in range(CHUNKS):
        at = pl.ds(i * rows, rows)
        copies.append((out_in.at[at], out.at[at], out_hbm.at[at]))
    inward = [pltpu.make_async_copy(c[0], c[1], isem.at[i]) for i, c in enumerate(copies)]
    outward = [pltpu.make_async_copy(c[1], c[2], osem.at[i]) for i, c in enumerate(copies)]
    for copy in inward:
        copy.start()
    for one, two in zip(inward, outward):
        one.wait()
        two.start()
    for copy in outward:
        copy.wait()


def finish(att, out):
    hbm = pl.BlockSpec(memory_space=pl.ANY)
    dma = pltpu.SemaphoreType.DMA
    return pl.pallas_call(
        finish_kernel,
        out_shape=tuple(jax.ShapeDtypeStruct(x.shape, x.dtype) for x in (att, out)),
        in_specs=[hbm] * 2,
        out_specs=(hbm,) * 2,
        scratch_shapes=[
            pltpu.VMEM(att.shape, BF),
            pltpu.VMEM(out.shape, BF),
            dma((CHUNKS + 1,)),
            dma((CHUNKS + 1,)),
        ],
        name="finish",
    )(att, out)


def per_device(activations, w_query, w_key, w_value, doc_lengths, block_dest, out_grad):
    ranks = lax.axis_size("ctx")
    nheads = lax.axis_size("heads")
    chips = nheads // 2
    rows, feat = activations.shape
    block = rows * ranks // block_dest.shape[0]
    cw = feat // CHUNKS
    wide = w_query.shape[1]
    half = w_key.shape[1]
    groups = half // HD
    reach = ranks // 4
    slots = 2 * reach + 1
    keys = slots * rows
    hbm = pl.BlockSpec(memory_space=pl.ANY)
    dma = pltpu.SemaphoreType.DMA
    att, out = pl.pallas_call(
        kernel,
        out_shape=(
            jax.ShapeDtypeStruct((rows, wide), BF),
            jax.ShapeDtypeStruct((rows, feat), BF),
        ),
        in_specs=[pl.BlockSpec(memory_space=pltpu.SMEM)] * 2 + [hbm] * 5,
        out_specs=(hbm, hbm),
        scratch_shapes=[
            pltpu.VMEM((nheads, CHUNKS, rows, cw), BF),
            pltpu.VMEM((rows, max(feat, wide + 2 * half)), F32),
            pltpu.VMEM((ranks, block, wide), BF),
            pltpu.VMEM((ranks, block, wide), BF),
            pltpu.VMEM((ranks, block, wide), BF),
            pltpu.VMEM((ranks, block, wide), BF),
            pltpu.VMEM(w_query.shape, BF),
            pltpu.VMEM(w_key.shape, BF),
            pltpu.VMEM(w_value.shape, BF),
            pltpu.VMEM((keys, 2 * half), BF),
            pltpu.VMEM((rows, wide), BF),
            pltpu.VMEM((rows, wide), BF),
            pltpu.VMEM((rows, keys), F32),
            pltpu.VMEM((rows, wide), BF),
            pltpu.VMEM((rows, wide), BF),
            pltpu.VMEM((keys, 2 * HD), F32),
            pltpu.VMEM((groups * QPK, rows, keys), F32),
            pltpu.VMEM((groups, HALVES, slots, rows // HALVES, 2 * HD), BF),
            pltpu.VMEM((groups, reach + 2, rows, 2 * HD), BF),
            pltpu.VMEM((groups, reach, rows, 2 * HD), BF),
            pltpu.VMEM((groups, reach, rows, 2 * HD), BF),
            pltpu.VMEM((rows, half), BF),
            pltpu.VMEM((rows, half), BF),
            pltpu.VMEM((chips - 1, CHUNKS, rows, cw), BF),
            pltpu.VMEM((chips - 1, CHUNKS, rows, cw), BF),
            dma((nheads, 3)),
            dma((CHUNKS,)),
            dma,
            dma,
            dma((HALVES, CHUNKS)),
            pltpu.SemaphoreType.REGULAR,
            dma((CHUNKS,)),
            dma((CHUNKS,)),
            dma((chips - 1, HALVES, CHUNKS)),
            dma((chips - 1, HALVES, CHUNKS)),
            dma((chips - 1, HALVES, CHUNKS)),
            dma((chips - 1, HALVES, CHUNKS)),
            dma((ranks,)),
            dma((ranks,)),
            dma((reach, HALVES)),
            dma((reach, HALVES)),
            dma((reach, HALVES)),
            dma((reach, HALVES)),
            dma((groups, reach, HALVES)),
            dma((groups, reach, HALVES)),
            dma((groups, reach, HALVES)),
            dma((groups, reach, HALVES)),
            dma((ranks,)),
            dma((ranks,)),
            dma((chips - 1, HALVES, CHUNKS)),
            dma((chips - 1, HALVES, CHUNKS)),
            dma((chips - 1, HALVES, CHUNKS)),
            dma((chips - 1, HALVES, CHUNKS)),
            dma((CHUNKS,)),
            dma((CHUNKS,)),
        ],
        compiler_params=pltpu.CompilerParams(
            vmem_limit_bytes=62 * 2**20, collective_id=1, has_side_effects=True
        ),
        name="attention",
    )(block_dest, doc_lengths, activations, out_grad, w_query, w_key, w_value)
    return finish(att, out)


def solution(mesh):
    return jax.shard_map(
        per_device,
        mesh=mesh,
        in_specs=(
            P("ctx", "heads"),
            P(None, "heads"),
            P(None, "heads"),
            P(None, "heads"),
            P(),
            P(),
            P("ctx", "heads"),
        ),
        out_specs=(P("ctx", "heads"), P("ctx", "heads")),
        check_vma=False,
    )
```

```python
import math

import jax
import jax.numpy as jnp
from jax import lax
from jax.experimental import pallas as pl
from jax.experimental.pallas import tpu as pltpu
from jax.sharding import PartitionSpec as P

HD = 128
QPK = 4
NEG = -1e30
SCALE = 1.0 / math.sqrt(HD)
LOG2E = 1.0 / math.log(2.0)
BF = jnp.bfloat16
F32 = jnp.float32
CHUNKS = 4
HALVES = 2


def dot_nt(a, b):
    return lax.dot_general(a, b, (((1,), (1,)), ((), ())), preferred_element_type=F32)


def dot_tn(a, b):
    return lax.dot_general(a, b, (((0,), (0,)), ((), ())), preferred_element_type=F32)


def dot_nn(a, b):
    return jnp.dot(a, b, preferred_element_type=F32)


def row_starts(len_ref, rank, rows):
    pos = rank * rows + lax.broadcasted_iota(jnp.int32, (rows, 1), 0)
    start = jnp.zeros((rows, 1), jnp.int32)
    end = 0
    for i in range(len_ref.shape[0]):
        end = end + len_ref[i]
        start = jnp.where(pos >= end, end, start)
    return start


def one_if(cond):
    return jnp.where(cond, 1.0, 0.0)


def arrivals(block_ref, rank, ranks):
    each = block_ref.shape[0] // ranks
    has = []
    for t in range(ranks):
        count = 0
        for k in range(each):
            count = count + jnp.where(block_ref[t * each + k] == rank, 1, 0)
        has.append(count)

    def place(target):
        return sum(jnp.where(t < target, has[t], 0) for t in range(ranks))

    return has, place


def bias_of(start, rank, keys):
    rows = start.shape[0]
    part = rows // HALVES
    qpos = rank * rows + lax.broadcasted_iota(jnp.int32, (rows, keys), 0)
    col = lax.broadcasted_iota(jnp.int32, (rows, keys), 1)
    later = col // (keys // HALVES)
    slot = (col - later * (keys // HALVES)) // part
    kpos = (rank - slot) * rows + later * part + lax.rem(col, part)
    seen = (kpos <= qpos) & (kpos >= start)
    return jnp.where(seen, 0.0, NEG)


def pick(source, block, wanted):
    total = None
    for b in range(source.shape[0] // block):
        term = source[b * block : (b + 1) * block, :].astype(F32) * wanted(b)
        total = term if total is None else total + term
    return total.astype(BF)


def split(h, kv_ref):
    half = kv_ref.shape[1] // 2
    g = h // QPK
    ks = slice(g * HD, (g + 1) * HD)
    vs = slice(half + g * HD, half + (g + 1) * HD)
    return slice(h * HD, (h + 1) * HD), ks, vs


def score(h, keys, w_ref, q_ref, kv_ref, bias_ref):
    hs, ks, _ = split(h, kv_ref)
    s = dot_nt(q_ref[:, hs], kv_ref[keys, ks])
    w_ref[h, :, keys] = s * (SCALE * LOG2E) + bias_ref[:, keys]


def attend(h, w_ref, kv_ref, att_ref):
    hs, _, vs = split(h, kv_ref)
    s = w_ref[h]
    m = jnp.max(s, axis=1, keepdims=True)
    p = jnp.exp2(s - m)
    w = p * (1.0 / jnp.sum(p, axis=1, keepdims=True))
    w_ref[h] = w
    att_ref[:, hs] = dot_nn(w.astype(BF), kv_ref[:, vs]).astype(BF)


def attend_back(h, w_ref, q_ref, kv_ref, g_ref, att_ref, dkv_ref):
    hs, _, vs = split(h, kv_ref)
    go = g_ref[:, hs]
    delta = jnp.sum(go.astype(F32) * att_ref[:, hs].astype(F32), axis=1, keepdims=True)
    w = w_ref[h]
    dv = dot_tn(w.astype(BF), go)
    ds = w * (dot_nt(go, kv_ref[:, vs]) - delta)
    w_ref[h] = ds
    dk = dot_tn(ds.astype(BF), q_ref[:, hs])
    if h % QPK == 0:
        dkv_ref[:, :HD] = dk
        dkv_ref[:, HD:] = dv
    else:
        dkv_ref[:, :HD] += dk
        dkv_ref[:, HD:] += dv


def attend_query(h, w_ref, kv_ref, dq_ref):
    hs, ks, _ = split(h, kv_ref)
    dq_ref[:, hs] = (dot_nn(w_ref[h].astype(BF), kv_ref[:, ks]) * SCALE).astype(BF)


def kernel(
    block_ref, len_ref, x_hbm, grad_hbm, wq_hbm, wk_hbm, wv_hbm,
    att_hbm, out_hbm,
    xall, acc, slots, outgo, got, back, wq, wk, wv, kv, q, g, bias, att, dq, sums, weights,
    send, xrx, zsend, zrx, dk, dv, pre_tx, far_tx,
    wsem, xsem, gsem, asem, osem, ready,
    ns, nr, fs, fr, gs, gr, asend, arecv, zs, zr, xs, xr,
    bxs, bxr, bzs, bzr, bsend, brecv, ps, pr, f2s, f2r, n2s, n2r,
):
    rank = lax.axis_index("ctx")
    head = lax.axis_index("heads")
    ranks = lax.axis_size("ctx")
    nheads = lax.axis_size("heads")
    core = lax.rem(head, 2)
    turn = 1 - 2 * core
    sib = head + turn
    chips = nheads // 2
    chip = head // 2
    side = lax.rem(rank, 2)
    pair = rank // 2
    pairs = ranks // 2
    mate = rank + 1 - 2 * side
    rows = q.shape[0]
    part = rows // HALVES
    width = xall.shape[3]
    feat = CHUNKS * width
    reach = ranks // 4
    nslots = 2 * reach + 1
    early = (nslots + 1) * part
    wide = q.shape[1]
    half = kv.shape[1] // 2
    groups = half // HD
    block = slots.shape[1]
    nblk = rows // block
    barrier = pltpu.get_barrier_semaphore()

    def to(ctx, h):
        return dict(device_id=(ctx, h), device_id_type=pl.DeviceIdType.MESH)

    def across(d):
        return lax.rem(chip + d, chips) * 2 + core

    def behind(d):
        return lax.rem(chip + chips - d, chips) * 2 + core

    def cut(a):
        return slice(a * part, (a + 1) * part)

    def cols(c):
        return pl.ds(pl.multiple_of(c * width, width), width)

    def piece(t, c):
        return pl.ds(pl.multiple_of(t * feat + c * width, width), width)

    def place_of(j, a):
        return pl.ds(pl.multiple_of((a * nslots + j) * part, part), part)

    def remote(src, dst, ssem, rsem, target):
        return pltpu.make_async_remote_copy(
            src_ref=src, dst_ref=dst, send_sem=ssem, recv_sem=rsem, **target
        )

    for o in range(1, ranks):
        pl.semaphore_signal(barrier, inc=1, **to(lax.rem(rank + o, ranks), head))
    for d in range(1, chips):
        pl.semaphore_signal(barrier, inc=1, **to(rank, across(d)))
    pl.semaphore_signal(barrier, inc=1, **to(rank, sib))

    def xload(c):
        return pltpu.make_async_copy(x_hbm.at[:, cols(c)], xall.at[head, c], xsem.at[c])

    gload = pltpu.make_async_copy(grad_hbm, att, gsem)
    order = [head, sib]
    for d in range(1, chips):
        order = order + [behind(d), behind(d) + turn]

    def loads(n):
        at = pl.ds(pl.multiple_of(order[n] * feat, feat), feat)
        return [
            pltpu.make_async_copy(s.at[at, :], t.at[at, :], wsem.at[n, i])
            for i, (s, t) in enumerate(((wq_hbm, wq), (wk_hbm, wk), (wv_hbm, wv)))
        ]

    gload.start()
    for c in range(CHUNKS):
        xload(c).start()
    for n in range(2):
        for load in loads(n):
            load.start()
    for d in range(1, reach + 1):
        @pl.when(pair < d)
        def _():
            for a in range(HALVES):
                kv[place_of(2 * d, a), :] = jnp.zeros((part, 2 * half), BF)

    @pl.when(pair + 1 == pairs)
    def _():
        zrx[...] = jnp.zeros_like(zrx)

    for gi in range(groups):
        xrx[gi, 0] = jnp.zeros(xrx.shape[2:], BF)
        xrx[gi, reach + 1] = jnp.zeros(xrx.shape[2:], BF)
    acc[...] = jnp.zeros_like(acc)
    pl.semaphore_wait(barrier, ranks + chips - 1)

    def far(d, a, c):
        return remote(
            x_hbm.at[cut(a), cols(c)], xall.at[head, c, cut(a)],
            fs.at[d - 1, a, c], fr.at[d - 1, a, c], to(rank, across(d)),
        )

    def near(c):
        return remote(
            x_hbm.at[:, cols(c)], xall.at[head, c], ns.at[c], nr.at[c], to(rank, sib)
        )

    def give(d, a, c):
        return remote(
            xall.at[behind(d), c, cut(a)], xall.at[behind(d), c, cut(a)],
            gs.at[d - 1, a, c], gr.at[d - 1, a, c], to(rank, sib),
        )

    for d in range(1, chips):
        for c in range(CHUNKS):
            far(d, 0, c).start()
    for n in range(2, nheads):
        for load in loads(n):
            load.start()
    for c in range(CHUNKS):
        near(c).start()

    def acopy(o):
        return remote(
            slots.at[o], got.at[rank], asend.at[o], arecv.at[o],
            to(lax.rem(rank + o, ranks), head),
        )

    def batch(o):
        if o % 4 == 2:
            return 2
        return 0

    def send_batch(n):
        for o in range(1, ranks):
            if batch(o) == n:
                acopy(o).start()

    has, place = arrivals(block_ref, rank, ranks)
    gload.wait()
    for o in range(ranks):
        spot = place(lax.rem(rank + o, ranks))
        value = pick(att, block, lambda b: one_if(spot == b))
        if o == 0:
            got[rank] = value
        else:
            slots[o] = value
            if batch(o) == 0:
                acopy(o).start()

    def add_kv(x, r, t, c):
        at = piece(t, c)
        acc[r, wide : wide + half] += dot_nn(x, wk[at, :])
        acc[r, wide + half : wide + 2 * half] += dot_nn(x, wv[at, :])

    def add_q(x, r, t, c):
        acc[r, :wide] += dot_nn(x, wq[piece(t, c), :])

    everyrow = slice(0, rows)
    for load in loads(0):
        load.wait()

    @pl.loop(0, CHUNKS)
    def _(c):
        xload(c).wait()
        add_kv(xall[head, c], everyrow, head, c)
        add_q(xall[head, c], everyrow, head, c)

    for load in loads(1):
        load.wait()

    @pl.loop(0, CHUNKS)
    def _(c):
        near(c).wait()
        add_kv(xall[sib, c], everyrow, sib, c)
        add_q(xall[sib, c], everyrow, sib, c)

    for n in range(2, nheads):
        for load in loads(n):
            load.wait()

    def zcopy(d, a):
        return remote(
            kv.at[place_of(2 * d - 2, a), :], kv.at[place_of(2 * d, a), :],
            zs.at[d - 1, a], zr.at[d - 1, a], to(rank + 2, head),
        )

    def xcopy(i, a):
        return remote(
            kv.at[place_of(2 * (i + side), a), :], kv.at[place_of(2 * i + 1, a), :],
            xs.at[i, a], xr.at[i, a], to(mate, head),
        )

    def kv_begin(a):
        kv[place_of(0, a), :] = acc[cut(a), wide : wide + 2 * half].astype(BF)

        @pl.when(pair + 1 < pairs)
        def _():
            zcopy(1, a).start()

        @pl.when(side == 0)
        def _():
            xcopy(0, a).start()

    def kv_step(d, a):
        @pl.when(pair >= d)
        def _():
            zcopy(d, a).wait_recv()

        if d < reach:
            @pl.when((pair >= d) & (pair + 1 < pairs))
            def _():
                zcopy(d + 1, a).start()

            @pl.when(side == 0)
            def _():
                xcopy(d, a).start()

        @pl.when(side == 1)
        def _():
            xcopy(d - 1, a).start()

    def kv_end(a):
        for i in range(reach):
            xcopy(i, a).wait()
        for d in range(1, reach + 1):
            @pl.when((pair >= d - 1) & (pair + 1 < pairs))
            def _():
                zcopy(d, a).wait_send()

    last = CHUNKS - 1
    for a in range(HALVES):
        for d in range(1, chips):
            one = behind(d)
            two = one + turn

            @pl.loop(0, CHUNKS)
            def _(c):
                far(d, a, c).wait()
                give(d, a, c).start()
                if a + 1 < HALVES:
                    far(d, a + 1, c).start()
                add_kv(xall[one, c, cut(a)], cut(a), one, c)

                @pl.when(c > 0)
                def _():
                    add_q(xall[one, c - 1, cut(a)], cut(a), one, c - 1)
                    add_q(xall[two, c - 1, cut(a)], cut(a), two, c - 1)

                give(d, a, c).wait()
                add_kv(xall[two, c, cut(a)], cut(a), two, c)
                if a > 0 and d == chips - 1:
                    for e in range(1, reach + 1):
                        @pl.when(c == e - 1)
                        def _():
                            kv_step(e, a - 1)

                    @pl.when(c == min(reach, last))
                    def _():
                        send_batch(1)

            if d == chips - 1:
                kv_begin(a)
            add_q(xall[one, last, cut(a)], cut(a), one, last)
            add_q(xall[two, last, cut(a)], cut(a), two, last)

    for d in range(1, chips):
        pl.semaphore_signal(ready, inc=1, **to(rank, across(d)))
    pl.semaphore_signal(ready, inc=1, **to(rank, sib))
    q[...] = acc[:, :wide].astype(BF)
    bias[...] = bias_of(row_starts(len_ref, rank, rows), rank, kv.shape[0])
    heads = range(groups * QPK)
    for a in range(HALVES - 1):
        kv_end(a)
    for h in heads:
        score(h, slice(0, early), weights, q, kv, bias)
        for d in range(1, reach + 1):
            if h == d * len(heads) // (2 * reach):
                kv_step(d, HALVES - 1)
    send_batch(2)
    kv_end(HALVES - 1)

    def assemble_grad():
        for o in range(1, ranks):
            acopy(o).wait()
        for b in range(nblk):
            target = block_ref[rank * nblk + b]
            total = jnp.zeros(slots.shape[1:], F32)
            for s in range(ranks):
                total = total + got[s].astype(F32) * one_if(target == s)
            g[b * block : (b + 1) * block, :] = total.astype(BF)

    def bx(gi, i, a):
        return remote(
            send.at[gi, a, 2 * i + 1], xrx.at[gi, i + 1, cut(a)],
            bxs.at[gi, i, a], bxr.at[gi, i, a], to(mate, head),
        )

    def bz(gi, d, a):
        return remote(
            zsend.at[gi, d - 1, cut(a)], zrx.at[gi, d - 1, cut(a)],
            bzs.at[gi, d - 1, a], bzr.at[gi, d - 1, a], to(rank - 2, head),
        )

    def dkv_begin(gi, a):
        for i in reversed(range(reach)):
            bx(gi, i, a).start()

    def put_dkv(gi):
        shape = send.shape[1:4] + (HD,)
        send[gi, :, :, :, :HD] = (sums[:, :HD] * SCALE).astype(BF).reshape(shape)
        send[gi, :, :, :, HD:] = sums[:, HD:].astype(BF).reshape(shape)
        dkv_begin(gi, 0)

    def level(gi, d, a):
        if d > 0:
            bx(gi, d - 1, a).wait()

        def whole():
            both = send[gi, a, 2 * d].astype(F32) + xrx[gi, d + 1 - side, cut(a)].astype(F32)
            if d < reach:
                both = both + zrx[gi, d, cut(a)].astype(F32)
            return both.astype(BF)

        if d < reach:
            @pl.when((pair >= d) & (pair + 1 < pairs))
            def _():
                bz(gi, d + 1, a).wait_recv()

        if d > 0:
            @pl.when(pair >= d)
            def _():
                zsend[gi, d - 1, cut(a)] = whole()
                bz(gi, d, a).start()
        else:
            total = whole()
            dk[cut(a), gi * HD : (gi + 1) * HD] = total[:, :HD]
            dv[cut(a), gi * HD : (gi + 1) * HD] = total[:, HD:]

    def bcopy(o):
        return remote(
            outgo.at[o], back.at[rank], bsend.at[o], brecv.at[o],
            to(lax.rem(rank + o, ranks), head),
        )

    def put_att(o):
        target = lax.rem(rank + o, ranks)
        value = pick(att, block, lambda b: one_if(block_ref[rank * nblk + b] == target))
        if o == 0:
            back[rank] = value
        else:
            outgo[o] = value

    for h in heads:
        score(h, slice(early, kv.shape[0]), weights, q, kv, bias)
        attend(h, weights, kv, att)
    for o in range(2, ranks, 2):
        put_att(o)
        bcopy(o).start()
    assemble_grad()
    for gi in range(groups):
        for i in range(QPK):
            attend_back(gi * QPK + i, weights, q, kv, g, att, sums)
        put_dkv(gi)
    def parked(t, c):
        n = t * CHUNKS + c
        per = kv.shape[0] // width
        return n // per, pl.ds(pl.multiple_of(lax.rem(n, per) * width, width), width)

    def query_part(t):
        @pl.loop(0, CHUNKS)
        def _(c):
            n, at = parked(t, c)
            weights[n, :, at] = dot_nt(dq[...], wq[piece(t, c), :])

    def levels(d, a):
        for gi in range(groups):
            level(gi, d, a)

    for h in heads:
        attend_query(h, weights, kv, dq)
        if h % QPK == QPK - 1:
            level(h // QPK, reach, 0)
    for a in range(1, HALVES):
        for gi in range(groups):
            dkv_begin(gi, a)
    for d in range(1, chips):
        query_part(across(d) + turn)
    for d in range(reach - 1, 0, -1):
        levels(d, 0)
    for d in range(1, chips):
        query_part(across(d))
    put_att(0)
    for o in range(1, ranks, 2):
        put_att(o)
    levels(0, 0)

    def term(t, c, r):
        at = piece(t, c)
        n, spot = parked(t, c)
        return weights[n, r, spot] + dot_nt(dk[r, :], wk[at, :]) + dot_nt(dv[r, :], wv[at, :])

    def pre(d, a, c):
        return remote(
            pre_tx.at[d - 1, c, cut(a)], xall.at[behind(d), c, cut(a)],
            ps.at[d - 1, a, c], pr.at[d - 1, a, c], to(rank, sib),
        )

    def far2(d, a, c):
        return remote(
            far_tx.at[d - 1, c, cut(a)], xall.at[head, c, cut(a)],
            f2s.at[d - 1, a, c], f2r.at[d - 1, a, c], to(rank, across(d)),
        )

    def near2(c):
        return remote(xall.at[head, c], xall.at[head, c], n2s.at[c], n2r.at[c], to(rank, sib))

    def others(a):
        for d in range(1, chips):
            def forward(c):
                mine = term(across(d), c, cut(a))
                pre(d, a, c).wait()
                mine = mine + xall[behind(d) + turn, c, cut(a)].astype(F32)
                far_tx[d - 1, c, cut(a)] = mine.astype(BF)
                far2(d, a, c).start()

            @pl.loop(0, CHUNKS)
            def _(c):
                pre_tx[d - 1, c, cut(a)] = term(across(d) + turn, c, cut(a)).astype(BF)
                pre(d, a, c).start()

                @pl.when(c > 0)
                def _():
                    forward(c - 1)

            forward(last)

    pl.semaphore_wait(ready, chips)
    others(0)
    for a in range(1, HALVES):
        levels(reach, a)
        query_part(sib)
        for d in range(reach - 1, 0, -1):
            levels(d, a)
        query_part(head)
        for o in range(1, ranks, 2):
            bcopy(o).start()
        levels(0, a)
        others(a)

    @pl.loop(0, CHUNKS)
    def _(c):
        xall[head, c] = term(sib, c, everyrow).astype(BF)
        near2(c).start()
        acc[:, cols(c)] = term(head, c, everyrow)

    for gi in range(groups):
        for d in range(1, reach + 1):
            for a in range(HALVES):
                @pl.when(pair >= d)
                def _():
                    bz(gi, d, a).wait_send()

    def store(a, c):
        return pltpu.make_async_copy(
            far_tx.at[0, c, cut(a)], out_hbm.at[cut(a), cols(c)], osem.at[a, c]
        )

    def finish_rows(a):
        @pl.loop(0, CHUNKS)
        def _(c):
            if a == 0:
                near2(c).wait()
            total = acc[cut(a), cols(c)] + xall[sib, c, cut(a)].astype(F32)
            for d in range(1, chips):
                far2(d, a, c).wait()
                total = total + xall[behind(d), c, cut(a)].astype(F32)
            far_tx[0, c, cut(a)] = total.astype(BF)
            store(a, c).start()

    for a in range(HALVES - 1):
        finish_rows(a)
    for o in range(1, ranks):
        bcopy(o).wait()
    spots = [place(t) for t in range(ranks)]
    for b in range(nblk):
        total = jnp.zeros(slots.shape[1:], F32)
        for t in range(ranks):
            total = total + back[t].astype(F32) * one_if((has[t] > 0) & (spots[t] == b))
        att[b * block : (b + 1) * block, :] = total.astype(BF)
    astore = pltpu.make_async_copy(att, att_hbm, asem)
    astore.start()
    finish_rows(HALVES - 1)
    astore.wait()
    for a in range(HALVES):
        for c in range(CHUNKS):
            store(a, c).wait()


def finish_kernel(att_in, out_in, att_hbm, out_hbm, att, out, isem, osem):
    rows = out_in.shape[0] // CHUNKS
    copies = [(att_in, att, att_hbm)]
    for i in range(CHUNKS):
        at = pl.ds(i * rows, rows)
        copies.append((out_in.at[at], out.at[at], out_hbm.at[at]))
    inward = [pltpu.make_async_copy(c[0], c[1], isem.at[i]) for i, c in enumerate(copies)]
    outward = [pltpu.make_async_copy(c[1], c[2], osem.at[i]) for i, c in enumerate(copies)]
    for copy in inward:
        copy.start()
    for one, two in zip(inward, outward):
        one.wait()
        two.start()
    for copy in outward:
        copy.wait()


def finish(att, out):
    hbm = pl.BlockSpec(memory_space=pl.ANY)
    dma = pltpu.SemaphoreType.DMA
    return pl.pallas_call(
        finish_kernel,
        out_shape=tuple(jax.ShapeDtypeStruct(x.shape, x.dtype) for x in (att, out)),
        in_specs=[hbm] * 2,
        out_specs=(hbm,) * 2,
        scratch_shapes=[
            pltpu.VMEM(att.shape, BF),
            pltpu.VMEM(out.shape, BF),
            dma((CHUNKS + 1,)),
            dma((CHUNKS + 1,)),
        ],
        name="finish",
    )(att, out)


def per_device(activations, w_query, w_key, w_value, doc_lengths, block_dest, out_grad):
    ranks = lax.axis_size("ctx")
    nheads = lax.axis_size("heads")
    chips = nheads // 2
    rows, feat = activations.shape
    block = rows * ranks // block_dest.shape[0]
    cw = feat // CHUNKS
    wide = w_query.shape[1]
    half = w_key.shape[1]
    groups = half // HD
    reach = ranks // 4
    slots = 2 * reach + 1
    keys = slots * rows
    hbm = pl.BlockSpec(memory_space=pl.ANY)
    dma = pltpu.SemaphoreType.DMA
    att, out = pl.pallas_call(
        kernel,
        out_shape=(
            jax.ShapeDtypeStruct((rows, wide), BF),
            jax.ShapeDtypeStruct((rows, feat), BF),
        ),
        in_specs=[pl.BlockSpec(memory_space=pltpu.SMEM)] * 2 + [hbm] * 5,
        out_specs=(hbm, hbm),
        scratch_shapes=[
            pltpu.VMEM((nheads, CHUNKS, rows, cw), BF),
            pltpu.VMEM((rows, max(feat, wide + 2 * half)), F32),
            pltpu.VMEM((ranks, block, wide), BF),
            pltpu.VMEM((ranks, block, wide), BF),
            pltpu.VMEM((ranks, block, wide), BF),
            pltpu.VMEM((ranks, block, wide), BF),
            pltpu.VMEM(w_query.shape, BF),
            pltpu.VMEM(w_key.shape, BF),
            pltpu.VMEM(w_value.shape, BF),
            pltpu.VMEM((keys, 2 * half), BF),
            pltpu.VMEM((rows, wide), BF),
            pltpu.VMEM((rows, wide), BF),
            pltpu.VMEM((rows, keys), F32),
            pltpu.VMEM((rows, wide), BF),
            pltpu.VMEM((rows, wide), BF),
            pltpu.VMEM((keys, 2 * HD), F32),
            pltpu.VMEM((groups * QPK, rows, keys), F32),
            pltpu.VMEM((groups, HALVES, slots, rows // HALVES, 2 * HD), BF),
            pltpu.VMEM((groups, reach + 2, rows, 2 * HD), BF),
            pltpu.VMEM((groups, reach, rows, 2 * HD), BF),
            pltpu.VMEM((groups, reach, rows, 2 * HD), BF),
            pltpu.VMEM((rows, half), BF),
            pltpu.VMEM((rows, half), BF),
            pltpu.VMEM((chips - 1, CHUNKS, rows, cw), BF),
            pltpu.VMEM((chips - 1, CHUNKS, rows, cw), BF),
            dma((nheads, 3)),
            dma((CHUNKS,)),
            dma,
            dma,
            dma((HALVES, CHUNKS)),
            pltpu.SemaphoreType.REGULAR,
            dma((CHUNKS,)),
            dma((CHUNKS,)),
            dma((chips - 1, HALVES, CHUNKS)),
            dma((chips - 1, HALVES, CHUNKS)),
            dma((chips - 1, HALVES, CHUNKS)),
            dma((chips - 1, HALVES, CHUNKS)),
            dma((ranks,)),
            dma((ranks,)),
            dma((reach, HALVES)),
            dma((reach, HALVES)),
            dma((reach, HALVES)),
            dma((reach, HALVES)),
            dma((groups, reach, HALVES)),
            dma((groups, reach, HALVES)),
            dma((groups, reach, HALVES)),
            dma((groups, reach, HALVES)),
            dma((ranks,)),
            dma((ranks,)),
            dma((chips - 1, HALVES, CHUNKS)),
            dma((chips - 1, HALVES, CHUNKS)),
            dma((chips - 1, HALVES, CHUNKS)),
            dma((chips - 1, HALVES, CHUNKS)),
            dma((CHUNKS,)),
            dma((CHUNKS,)),
        ],
        compiler_params=pltpu.CompilerParams(
            vmem_limit_bytes=62 * 2**20, collective_id=1, has_side_effects=True
        ),
        name="attention",
    )(block_dest, doc_lengths, activations, out_grad, w_query, w_key, w_value)
    return finish(att, out)


def solution(mesh):
    return jax.shard_map(
        per_device,
        mesh=mesh,
        in_specs=(
            P("ctx", "heads"),
            P(None, "heads"),
            P(None, "heads"),
            P(None, "heads"),
            P(),
            P(),
            P("ctx", "heads"),
        ),
        out_specs=(P("ctx", "heads"), P("ctx", "heads")),
        check_vma=False,
    )
```
